32 devices in a mesh: ang: 8 (over y, x, core), ax: 4 (over z).
Axes of the slice: x: 2, y: 2, z: 4, core: 2. Of those that a mesh axis runs over, the one named last changes fastest.
Arguments:
- conserved: float32 [5, 96, 256, 256], P(None, 'ax', 'ang'), may hold values from -0.3 to 3.5, as said below
- deriv_matrix: float32 [512, 512], replicated, may hold values from -1 to 1
- filter_matrix: float32 [512, 512], replicated, may hold values from 0 to 1
Outputs:
- advanced: float32 [5, 96, 256, 256], P(None, 'ax', 'ang')
The draws below stay inside these ranges and needn't reach their ends.
Inputs may be any that keep to these rules, and one draw needn't show every extreme that they name: `conserved`: component 0 (density) lies in 0.8 to 1.2, components 1 to 3 (momenta) in -0.3 to 0.3, and the energy exceeds the kinetic energy by 1.75 to 3.25.
All inputs are finite; a program needn't handle non-finite values.
Results may differ from the reference program's by a relative error of at most 0.0003.
Values sent between devices are 32-bit elements; how exact they have to be, the bound alone decides.
No kernel may reach another device: no remote copies, remote signals or barrier semaphores. Data moves between devices by JAX's collectives and lax.ppermute only.
A program may use at most 128 MiB of HBM per device.

```python
import math
import jax
import jax.numpy as jnp
from jax import lax

R = 256
NA = 256
NZ = 96


def draw_conserved(key, part):
    key_list = jax.random.split(jax.random.fold_in(key, 11), 10)
    grid_shape = (NZ, NA, R)

    def uniform_field(index):
        return jax.random.uniform(key_list[index], grid_shape, jnp.float32)
    density = 0.8 + 0.4 * uniform_field(0)
    x_mom = 0.6 * uniform_field(2) - 0.3
    y_mom = 0.6 * uniform_field(4) - 0.3
    z_mom = 0.6 * uniform_field(6) - 0.3
    pressure = 0.7 + 0.6 * uniform_field(8)
    energy = pressure / 0.4 + 0.5 * (x_mom * x_mom + y_mom * y_mom + z_mom * z_mom) / density
    return jnp.stack([density, x_mom, y_mom, z_mom, energy]).astype(jnp.float32)


def draw_deriv_matrix(key, part):
    line_length = 2 * R
    index_grid = jnp.arange(line_length, dtype=jnp.float32)
    distance = jnp.abs(index_grid[:, None] - index_grid[None, :])
    raw_entries = jax.random.normal(jax.random.fold_in(key, 21), (line_length, line_length), jnp.float32)
    shaped = raw_entries * jnp.exp(-distance / (0.5 * R))
    return shaped / jnp.sqrt(jnp.sum(shaped * shaped, axis=1, keepdims=True))


def draw_filter_matrix(key, part):
    line_length = 2 * R
    index_grid = jnp.arange(line_length, dtype=jnp.float32)
    distance = jnp.abs(index_grid[:, None] - index_grid[None, :])
    uniform_raw = jax.random.uniform(jax.random.fold_in(key, 31), (line_length, line_length), jnp.float32)
    spiky = jnp.power(uniform_raw, 8.0)
    weights = spiky * jnp.exp(-distance / R) + 1e-06
    averaging = weights / jnp.sum(weights, axis=1, keepdims=True)
    return 0.5 * jnp.eye(line_length, dtype=jnp.float32) + 0.5 * averaging


def setup_inputs(seed: int = 0) -> dict:
    streams_of = jax.random.split(jax.random.key(seed), 4)
    return {
        "conserved": draw_conserved(jax.random.fold_in(streams_of[3], 71), 0),
        "deriv_matrix": draw_deriv_matrix(jax.random.fold_in(streams_of[3], 71), 0),
        "filter_matrix": draw_filter_matrix(jax.random.fold_in(streams_of[3], 71), 0),
    }


gamma_ratio = 1.4
courant = 0.15
highest = lax.Precision.HIGHEST


def flux_sets(conserved, cosine, sine_wave, radius):
    density = conserved[0]
    x_mom = conserved[1]
    y_mom = conserved[2]
    z_mom = conserved[3]
    energy = conserved[4]
    x_speed = x_mom / density
    y_speed = y_mom / density
    z_speed = z_mom / density
    pressure = (gamma_ratio - 1.0) * (energy - 0.5 * (x_mom * x_speed + y_mom * y_speed + z_mom * z_speed))
    radial_speed = x_speed * cosine + y_speed * sine_wave
    swirl_speed = y_speed * cosine - x_speed * sine_wave
    enthalpy = energy + pressure
    radial = jnp.stack([density * radial_speed, x_mom * radial_speed + pressure * cosine,
                        y_mom * radial_speed + pressure * sine_wave, z_mom * radial_speed,
                        enthalpy * radial_speed]) * radius
    angular = jnp.stack([density * swirl_speed, x_mom * swirl_speed - pressure * sine_wave,
                         y_mom * swirl_speed + pressure * cosine, z_mom * swirl_speed,
                         enthalpy * swirl_speed])
    axial = jnp.stack([z_mom, x_mom * z_speed, y_mom * z_speed, z_mom * z_speed + pressure,
                       enthalpy * z_speed])
    return radial, angular, axial


def central(values, axis_number):
    length = values.shape[axis_number] - 4

    def pick_plane(offset):
        return lax.slice_in_dim(values, 2 + offset, 2 + offset + length, axis=axis_number)

    return (8.0 * (pick_plane(1) - pick_plane(-1)) - (pick_plane(2) - pick_plane(-2))) / 12.0


def diameter(values, matrix, parity):
    half_cycle = values.shape[2] // 2
    radii_count = values.shape[3]
    lower_half = values[:, :, :half_cycle]
    upper_half = values[:, :, half_cycle:]
    diameter_line = jnp.concatenate([upper_half[..., ::-1], lower_half], axis=3)
    mapped = jnp.einsum("fzas,rs->fzar", diameter_line, matrix, precision=highest)
    return jnp.concatenate([mapped[..., radii_count:], parity * mapped[..., :radii_count][..., ::-1]], axis=2)


def reference(conserved, deriv_matrix, filter_matrix):
    angle_grid = jnp.arange(NA, dtype=jnp.int32).astype(jnp.float32) * (2.0 * math.pi / NA)
    cosine = jnp.cos(angle_grid)[:, None]
    sine_wave = jnp.sin(angle_grid)[:, None]
    radius = ((jnp.arange(R, dtype=jnp.int32).astype(jnp.float32) + 0.5) / R)[None, None, :]
    twist = NA / (2.0 * math.pi * R)
    block_planes = math.gcd(NZ, 8)
    block_count = NZ // block_planes

    def section(base_state, current, weight):
        padded = jnp.pad(current, ((0, 0), (2, 2), (0, 0), (0, 0)), mode="edge")

        def one_block(block_index):
            start = (block_index * block_planes).astype(jnp.int32)
            window = lax.dynamic_slice_in_dim(padded, start, block_planes + 4, axis=1)
            own_base = lax.dynamic_slice_in_dim(base_state, start, block_planes, axis=1)
            radial, angular, axial = flux_sets(window, cosine, sine_wave, radius)
            plane_index = start - 2 + jnp.arange(block_planes + 4, dtype=jnp.int32)
            inside = ((plane_index >= 0) & (plane_index < NZ)).astype(jnp.float32)[None, :, None, None]
            axial = axial * inside
            radial = radial[:, 2:-2]
            angular = angular[:, 2:-2]
            ang_pad = jnp.concatenate([angular[:, :, -2:], angular, angular[:, :, :2]], axis=2)
            local = own_base - (weight * courant) * (twist * central(ang_pad, 2) + radius * central(axial, 1))
            moved = local - (weight * courant) * diameter(radial, deriv_matrix, -1.0)
            return diameter(moved, filter_matrix, 1.0)

        blocks = lax.map(one_block, jnp.arange(block_count, dtype=jnp.int32))
        return jnp.moveaxis(blocks, 0, 1).reshape(5, NZ, NA, R)

    first = section(conserved, conserved, 1.0)
    return section(0.5 * conserved + 0.5 * first, first, 0.5)
```

```python
import functools
import math

import jax
import jax.numpy as jnp
from jax import lax
from jax.experimental import pallas as pl
from jax.experimental.pallas import tpu as pltpu
from jax.sharding import PartitionSpec as P

gamma_ratio = 1.4
courant = 0.15
highest = lax.Precision.HIGHEST
CHUNKS = 1


def split_kernel(w_ref, hi_ref, lo_ref):
    w = w_ref[...]
    hi = w.astype(jnp.bfloat16)
    hi_ref[...] = hi
    lo_ref[...] = (w - hi.astype(jnp.float32)).astype(jnp.bfloat16)


def split_weights(w):
    shape = jax.ShapeDtypeStruct(w.shape, jnp.bfloat16)
    return pl.pallas_call(split_kernel, out_shape=(shape, shape), name="split_weights")(w)


def speeds(q):
    rho, mx, my, mz, en = q
    inv = 1.0 / rho
    ux, uy, uz = mx * inv, my * inv, mz * inv
    pressure = (gamma_ratio - 1.0) * (en - 0.5 * (mx * ux + my * uy + mz * uz))
    return ux, uy, uz, pressure, en + pressure


def angular_of(q, state, cos, sin):
    rho, mx, my, mz, en = q
    ux, uy, uz, pressure, enthalpy = state
    us = uy * cos - ux * sin
    return (rho * us, mx * us - pressure * sin, my * us + pressure * cos, mz * us, enthalpy * us)


def radial_of(q, state, cos, sin, scale):
    rho, mx, my, mz, en = q
    ux, uy, uz, pressure, enthalpy = state
    ur = (ux * cos + uy * sin) * scale
    ps = pressure * scale
    return (rho * ur, mx * ur + ps * cos, my * ur + ps * sin, mz * ur, enthalpy * ur)


def axial_of(q, state):
    rho, mx, my, mz, en = q
    ux, uy, uz, pressure, enthalpy = state
    return (mz, mx * uz, my * uz, mz * uz + pressure, enthalpy * uz)


def section_kernel(
    dims, weight, twist, mixed,
    flags_ref, trig_ref, edge_trig_ref, radius_ref, q_ref, prev_ref, next_ref,
    left_ref, right_ref, base_ref, whi_ref, wlo_ref,
    out_ref, axial_s, part_s, ang_s, hi_s, lo_s,
):
    fields, planes, rows, radii = dims
    factor = weight * courant
    lane_halves = radii // 128
    ang_factor = factor * twist / 12.0

    def store_lhs(f, p, column, value):
        hi = value.astype(jnp.bfloat16)
        hi_s[f, p, :, column : column + radii] = hi
        lo_s[f, p, :, column : column + radii] = (value - hi.astype(jnp.float32)).astype(jnp.bfloat16)

    for s in range(2):
        for side, ref in ((0, prev_ref), (1, next_ref)):
            for k in range(2):
                q = tuple(ref[s, f, k] for f in range(fields))
                axial = axial_of(q, speeds(q))
                at = k + side * (planes + 2)
                for f in range(fields):
                    axial_s[s, f, at] = jnp.where(flags_ref[side] > 0, axial[f], 0.0)

    def first_pass(p, carry):
        edge = []
        for side, ref in ((0, left_ref), (1, right_ref)):
            q = tuple(ref[f, p] for f in range(fields))
            edge.append(angular_of(q, speeds(q), edge_trig_ref[0, side], edge_trig_ref[1, side]))
        scale = -factor * radius_ref[...]
        for s in range(2):
            q = tuple(q_ref[s, f, p] for f in range(fields))
            state = speeds(q)
            cos, sin = trig_ref[0, s], trig_ref[1, s]
            axial = axial_of(q, state)
            radial = radial_of(q, state, cos, sin, scale)
            angular = angular_of(q, state, cos, sin)
            for f in range(fields):
                axial_s[s, f, p + 2] = axial[f]
                store_lhs(f, p, 2 * radii + s * radii, radial[f])
                for l in range(lane_halves):
                    lanes = slice(l * 128, l * 128 + 128)
                    ang_s[s, f, l, 8 : 8 + rows] = angular[f][:, lanes]
                    ang_s[s, f, l, 6:8] = edge[0][f][2 * s : 2 * s + 2, lanes]
                    ang_s[s, f, l, 8 + rows : 10 + rows] = edge[1][f][2 * s : 2 * s + 2, lanes]
            for f in range(fields):
                for l in range(lane_halves):
                    lanes = slice(l * 128, l * 128 + 128)

                    def at(k):
                        return ang_s[s, f, l, 8 + k : 8 + k + rows]

                    slope = 8.0 * (at(1) - at(-1)) - (at(2) - at(-2))
                    own = q_ref[s, f, p, :, lanes]
                    if mixed:
                        own = 0.5 * base_ref[s, f, p, :, lanes] + 0.5 * own
                    part_s[s, f, p, :, lanes] = own - ang_factor * slope
        return carry

    lax.fori_loop(0, planes, first_pass, 0)

    def second_pass(p, carry):
        scale = (factor / 12.0) * radius_ref[...]
        for s in range(2):
            for f in range(fields):
                slope = 8.0 * (axial_s[s, f, p + 3] - axial_s[s, f, p + 1]) - (
                    axial_s[s, f, p + 4] - axial_s[s, f, p]
                )
                store_lhs(f, p, s * radii, part_s[s, f, p] - scale * slope)
        return carry

    lax.fori_loop(0, planes, second_pass, 0)

    def mapped(hi, lo, s):
        columns = slice(s * radii, s * radii + radii)
        whi = whi_ref[:, columns]
        dot = functools.partial(jnp.dot, preferred_element_type=jnp.float32)
        return dot(hi, whi) + dot(lo, whi) + dot(hi, wlo_ref[:, columns])

    if planes * rows >= 256:
        def one_field(f, carry):
            hi = hi_s[f].reshape(planes * rows, 4 * radii)
            lo = lo_s[f].reshape(planes * rows, 4 * radii)
            for s in range(2):
                out_ref[s, f] = mapped(hi, lo, s).reshape(planes, rows, radii)
            return carry

        lax.fori_loop(0, fields, one_field, 0)
    else:
        hi = hi_s[...].reshape(fields * planes * rows, 4 * radii)
        lo = lo_s[...].reshape(fields * planes * rows, 4 * radii)
        for s in range(2):
            out_ref[s] = mapped(hi, lo, s).reshape(fields, planes, rows, radii)


def section_chunk(consts, weight, twist, flags, q, prev, next_, left, right, base, name):
    trig, edge_trig, radius, whi, wlo = consts
    _, fields, planes, rows, radii = q.shape
    mixed = base is not None
    whole = pl.BlockSpec(memory_space=pltpu.VMEM)
    lines = fields * planes * rows

    def two_planes(array, last):
        at = array.shape[2] // 2 - 1 if last else 0
        return pl.BlockSpec((2, fields, 2, rows, radii), lambda i: (0, 0, at, 0, 0))

    def full(array):
        zeros = (0,) * array.ndim
        return pl.BlockSpec(array.shape, lambda i: zeros)

    if not mixed:
        base = radius
    return pl.pallas_call(
        functools.partial(section_kernel, (fields, planes, rows, radii), weight, twist, mixed),
        grid=(1,),
        out_shape=jax.ShapeDtypeStruct(q.shape, jnp.float32),
        in_specs=[
            pl.BlockSpec(memory_space=pltpu.SMEM), full(trig), full(edge_trig), full(radius), full(q),
            two_planes(prev, True), two_planes(next_, False), full(left), full(right), full(base),
            full(whi), full(wlo),
        ],
        out_specs=full(q),
        scratch_shapes=[
            pltpu.VMEM((2, fields, planes + 4, rows, radii), jnp.float32),
            pltpu.VMEM((2, fields, planes, rows, radii), jnp.float32),
            pltpu.VMEM((2, fields, radii // 128, rows + 16, 128), jnp.float32),
            pltpu.VMEM((fields, planes, rows, 4 * radii), jnp.bfloat16),
            pltpu.VMEM((fields, planes, rows, 4 * radii), jnp.bfloat16),
        ],
        cost_estimate=pl.CostEstimate(
            flops=2 * lines * 4 * radii * 2 * radii * 3, bytes_accessed=8 * lines * radii * 4,
            transcendentals=0,
        ),
        name=name,
    )(flags, trig, edge_trig, radius, q, prev, next_, left, right, base, whi, wlo)


def folded(matrix, radii):
    tall = jnp.concatenate([matrix[radii:], matrix[:radii][::-1]], axis=0)
    return jnp.concatenate([tall[:, radii:], tall[:, :radii][:, ::-1]], axis=1)


def per_device(conserved, deriv_matrix, filter_matrix):
    n = lax.axis_size("ang")
    count = lax.axis_size("ax")
    fields, planes, ang_dev, radii = conserved.shape
    rows = ang_dev // 2
    half = n // 2
    total = ang_dev * n
    twist = total / (2.0 * math.pi * radii)
    pos = lax.axis_index("ang")
    h, j, c = pos // half, (pos % half) // 2, pos % 2
    ring = 4 * j + 2 * (h ^ (j & 1)) + c
    keeps = h == (c ^ (j & 1))

    def dev(hh, jj, cc):
        return hh * half + 2 * jj + cc

    spots = [(hh, jj, cc) for hh in range(2) for jj in range(n // 4) for cc in range(2)]
    givers = [(hh, jj, cc) for hh, jj, cc in spots if hh != (cc ^ (jj & 1))]
    keepers = [(hh, jj, cc) for hh, jj, cc in spots if hh == (cc ^ (jj & 1))]
    to_even = [(dev(*g), dev(1 - g[0], g[1], 0)) for g in givers]
    to_odd = [(dev(*g), dev(1 - g[0], g[1], 1)) for g in givers]
    to_core = [(dev(*k), dev(k[0], k[1], 1 - k[2])) for k in keepers]
    order = [dev((r % 4 // 2) ^ (r // 4 & 1), r // 4, r % 2) for r in range(n)]
    to_left = [(order[r], order[(r - 1) % n]) for r in range(n)]
    to_right = [(order[r], order[(r + 1) % n]) for r in range(n)]
    up = [(i, i + 1) for i in range(count - 1)]
    down = [(i + 1, i) for i in range(count - 1)]

    def back(table):
        return [(b, a) for a, b in table]

    def angles(offsets):
        index = (ring * rows + offsets) % total
        return index.astype(jnp.float32) * (2.0 * math.pi / total)

    seg = jnp.arange(2, dtype=jnp.int32)[:, None] * (total // 2)
    centre = angles(seg + jnp.arange(rows, dtype=jnp.int32))
    left_rows = angles((seg + jnp.arange(-2, 0, dtype=jnp.int32)).reshape(4))
    right_rows = angles((seg + jnp.arange(rows, rows + 2, dtype=jnp.int32)).reshape(4))
    edges = jnp.stack([left_rows, right_rows])

    def spread(values):
        return jnp.broadcast_to(values[..., None], values.shape + (radii,))

    trig = spread(jnp.stack([jnp.cos(centre), jnp.sin(centre)]))
    edge_trig = spread(jnp.stack([jnp.cos(edges), jnp.sin(edges)]))
    radius = ((jnp.arange(radii, dtype=jnp.int32).astype(jnp.float32) + 0.5) / radii)[None]
    signs = jnp.where(jnp.arange(2 * radii, dtype=jnp.int32) < radii, -1.0, 1.0).astype(jnp.float32)
    composite = jnp.dot(filter_matrix, signs[:, None] * deriv_matrix, precision=highest)
    weights = jnp.concatenate(
        [folded(filter_matrix, radii).T, folded(composite, radii).T], axis=0
    )
    whi, wlo = split_weights(weights)
    consts = (trig, edge_trig, radius, whi, wlo)

    chunks = CHUNKS
    step = planes // chunks
    layer = lax.axis_index("ax")
    low_ok = (layer > 0).astype(jnp.int32)
    high_ok = (layer < count - 1).astype(jnp.int32)
    one = jnp.ones((), jnp.int32)

    def take(k):
        block = lax.slice_in_dim(conserved, k * step, (k + 1) * step, axis=1)
        first_half, second_half = block[:, :, :rows], block[:, :, rows:]
        from_even = lax.ppermute(first_half, "ang", to_even)
        from_odd = lax.ppermute(second_half, "ang", to_odd)
        own = jnp.where(c == 0, first_half, second_half)
        other = jnp.where(c == 0, second_half, first_half)
        near = jnp.where(keeps, own, lax.ppermute(other, "ang", to_core))
        far = jnp.where(c == 0, from_even, from_odd)
        return jnp.stack([jnp.where(h == 0, near, far), jnp.where(h == 0, far, near)])

    def edge_rows(q, start, swap):
        piece = q[:, :, :, start : start + 2]
        pair = (piece[0], piece[1])
        return jnp.concatenate(
            [jnp.where(swap, pair[1], pair[0]), jnp.where(swap, pair[0], pair[1])], axis=2
        )

    def halos(q):
        left = lax.ppermute(edge_rows(q, rows - 2, ring == n - 1), "ang", to_right)
        right = lax.ppermute(edge_rows(q, 0, ring == 0), "ang", to_left)
        return left, right

    def section(qs, bases, weight, name):
        sides = [halos(q) for q in qs]
        low = lax.ppermute(qs[-1][:, :, step - 2 :], "ax", up)
        high = lax.ppermute(qs[0][:, :, :2], "ax", down)
        outs = []
        for k in range(chunks):
            flags = jnp.stack([low_ok if k == 0 else one, high_ok if k == chunks - 1 else one])
            outs.append(
                section_chunk(
                    consts, weight, twist, flags, qs[k],
                    low if k == 0 else qs[k - 1], high if k == chunks - 1 else qs[k + 1],
                    sides[k][0], sides[k][1], None if bases is None else bases[k], name,
                )
            )
        return outs

    def give_back(q):
        near = jnp.where(h == 0, q[0], q[1])
        far = jnp.where(h == 0, q[1], q[0])
        even = lax.ppermute(far, "ang", back(to_even))
        odd = lax.ppermute(far, "ang", back(to_odd))
        core = lax.ppermute(near, "ang", back(to_core))
        first_half = jnp.where(keeps, jnp.where(c == 0, near, core), even)
        second_half = jnp.where(keeps, jnp.where(c == 0, core, near), odd)
        return jnp.concatenate([first_half, second_half], axis=2)

    qs = [take(k) for k in range(chunks)]
    first = section(qs, None, 1.0, "section_one")
    advanced = section(first, qs, 0.5, "section_two")
    return jnp.concatenate([give_back(q) for q in advanced], axis=1)


def solution(mesh):
    placed = (P(None, "ax", "ang", None), P(), P())
    return jax.shard_map(
        per_device,
        mesh=mesh,
        in_specs=placed,
        out_specs=P(None, "ax", "ang", None),
        check_vma=False,
    )
```

```python
import functools
import math

import jax
import jax.numpy as jnp
from jax import lax
from jax.experimental import pallas as pl
from jax.experimental.pallas import tpu as pltpu
from jax.sharding import PartitionSpec as P

gamma_ratio = 1.4
courant = 0.15
highest = lax.Precision.HIGHEST
anywhere = pl.BlockSpec(memory_space=pl.ANY)
scalars = pl.BlockSpec(memory_space=pltpu.SMEM)
vector = pl.BlockSpec(memory_space=pltpu.VMEM)
GROUP = 4


def split_kernel(w_ref, hi_ref, lo_ref):
    w = w_ref[...]
    hi = w.astype(jnp.bfloat16)
    hi_ref[...] = hi
    lo_ref[...] = (w - hi.astype(jnp.float32)).astype(jnp.bfloat16)


def split_weights(w):
    shape = jax.ShapeDtypeStruct(w.shape, jnp.bfloat16)
    return pl.pallas_call(split_kernel, out_shape=(shape, shape), name="split_weights")(w)


def speeds(q):
    rho, mx, my, mz, en = q
    inv = 1.0 / rho
    ux, uy, uz = mx * inv, my * inv, mz * inv
    pressure = (gamma_ratio - 1.0) * (en - 0.5 * (mx * ux + my * uy + mz * uz))
    return ux, uy, uz, pressure, en + pressure


def angular_of(q, state, cos, sin):
    rho, mx, my, mz, en = q
    ux, uy, uz, pressure, enthalpy = state
    us = uy * cos - ux * sin
    return (rho * us, mx * us - pressure * sin, my * us + pressure * cos, mz * us, enthalpy * us)


def radial_of(q, state, cos, sin, scale):
    rho, mx, my, mz, en = q
    ux, uy, uz, pressure, enthalpy = state
    ur = (ux * cos + uy * sin) * scale
    ps = pressure * scale
    return (rho * ur, mx * ur + ps * cos, my * ur + ps * sin, mz * ur, enthalpy * ur)


def axial_of(q, state, scale):
    rho, mx, my, mz, en = q
    ux, uy, uz, pressure, enthalpy = state
    uz = uz * scale
    return (mz * scale, mx * uz, my * uz, mz * uz + pressure * scale, enthalpy * uz)


def merged(sources):
    spans = []
    for array, at in sources:
        if spans and spans[-1][0] == array and spans[-1][1] + spans[-1][2] == at:
            spans[-1][2] += 1
        else:
            spans.append([array, at, 1])
    return spans


def run_copies(copies):
    for copy in copies:
        copy.start()


def wait_copies(copies):
    for copy in copies:
        copy.wait()


def section_kernel(plan, factor, *refs):
    fields, rows, radii = plan["dims"]
    lengths, mixed, final = plan["lengths"], plan["mixed"], plan["final"]
    total = sum(lengths)
    counts = plan["counts"]
    refs = list(refs)
    flags_ref, trig_ref, edge_trig_ref, radius_ref, whi_hbm, wlo_hbm = refs[:6]
    del refs[:6]
    groups = []
    for count in counts:
        groups.append(refs[:count])
        del refs[:count]
    q_in, base_in, left_in, right_in = groups
    outs = refs[: plan["outs"]]
    del refs[: plan["outs"]]
    q_s, base_s, left_s, right_s, whi_s, wlo_s, axial_s, ang_s, hi_s, lo_s, res_s, sems = refs
    lane_halves = radii // 128

    used = [0]

    def copy(src, dst):
        used[0] += 1
        return pltpu.make_async_copy(src, dst, sems.at[used[0] - 1])

    def gathered(spans_of_runs, sources, target):
        made, at = [], 0
        for spans in spans_of_runs:
            for array, start, count in spans:
                source = sources[array]
                if len(source.shape) == 5:
                    made.append(copy(source.at[:, :, start : start + count], target.at[:, :, at : at + count]))
                else:
                    made.append(copy(source.at[:, start : start + count], target.at[:, at : at + count]))
                at += count
        return made

    early = gathered(plan["q"], q_in, q_s)
    early += gathered(plan["left"], left_in, left_s) + gathered(plan["right"], right_in, right_s)
    base_copies = gathered(plan["base"], base_in, base_s) if mixed else []
    weight_copies = [copy(whi_hbm, whi_s), copy(wlo_hbm, wlo_s)]
    run_copies(early)
    run_copies(base_copies)
    run_copies(weight_copies)
    wait_copies(early)
    wait_copies(base_copies)

    axial_scale = (factor / 12.0) * radius_ref[...]
    radial_scale = -factor * radius_ref[...]

    def put(u, f, column, value):
        lanes = slice(column, column + value.shape[-1])
        hi = value.astype(jnp.bfloat16)
        hi_s[u, f, :, lanes] = hi
        lo_s[u, f, :, lanes] = (value - hi.astype(jnp.float32)).astype(jnp.bfloat16)

    def flux(at, u, flag):
        inner = u is not None
        if inner:
            slot = u % 3
            edge = []
            for side, ref in ((0, left_s), (1, right_s)):
                q = tuple(ref[f, u] for f in range(fields))
                edge.append(angular_of(q, speeds(q), edge_trig_ref[0, side], edge_trig_ref[1, side]))
        for s in range(2):
            q = tuple(q_s[s, f, at] for f in range(fields))
            state = speeds(q)
            axial = axial_of(q, state, axial_scale)
            for f in range(fields):
                value = axial[f]
                if flag is not None:
                    value = jnp.where(flags_ref[flag] > 0, value, 0.0)
                axial_s[s, f, at] = value
            if not inner:
                continue
            radial = radial_of(q, state, trig_ref[0, s], trig_ref[1, s], radial_scale)
            for f in range(fields):
                put(u, f, 2 * radii + s * radii, radial[f])
            angular = angular_of(q, state, trig_ref[2, s], trig_ref[3, s])
            for f in range(fields):
                for l in range(lane_halves):
                    lanes = slice(l * 128, l * 128 + 128)
                    ang_s[slot, s, f, l, 8 : 8 + rows] = angular[f][:, lanes]
                    ang_s[slot, s, f, l, 6:8] = edge[0][f][2 * s : 2 * s + 2, lanes]
                    ang_s[slot, s, f, l, 8 + rows : 10 + rows] = edge[1][f][2 * s : 2 * s + 2, lanes]

    def finish(at, u):
        slot = u % 3
        for s in range(2):
            for f in range(fields):
                for l in range(lane_halves):
                    lanes = slice(l * 128, l * 128 + 128)

                    def ang(k):
                        return ang_s[slot, s, f, l, 8 + k : 8 + k + rows]

                    def axi(k):
                        return axial_s[s, f, at + k, :, lanes]

                    near = (ang(1) - ang(-1)) + (axi(1) - axi(-1))
                    far = (ang(2) - ang(-2)) + (axi(2) - axi(-2))
                    own = q_s[s, f, at, :, lanes]
                    if mixed:
                        own = 0.5 * base_s[s, f, u, :, lanes] + 0.5 * own
                    put(u, f, s * radii + l * 128, (own - 8.0 * near) + far)

    half_at = flags_ref[3]
    left_swap, right_swap = flags_ref[2], flags_ref[4]
    out_copies = []

    def multiply(first, count):
        hi = hi_s[first : first + count].reshape(count * fields * rows, 4 * radii)
        lo = lo_s[first : first + count].reshape(count * fields * rows, 4 * radii)
        dot = functools.partial(jnp.dot, preferred_element_type=jnp.float32)
        for s in range(2):
            columns = slice(s * radii, s * radii + radii)
            whi = whi_s[:, columns]
            res = dot(hi, whi) + dot(lo, whi) + dot(hi, wlo_s[:, columns])
            where = jnp.bitwise_xor(half_at, s) if final else s
            for i in range(count):
                for f in range(fields):
                    start = (i * fields + f) * rows
                    res_s[where, f, first + i] = res[start : start + rows]
        if final:
            pieces = [(res_s.at[0], outs[0]), (res_s.at[1], outs[1])]
            for source, target in pieces:
                out_copies.append(
                    copy(source.at[:, first : first + count], target.at[:, first : first + count])
                )
        else:
            out_copies.append(
                copy(res_s.at[:, :, first : first + count], outs[0].at[:, :, first : first + count])
            )
            for i in range(first, first + count):
                for f in range(fields):
                    for ref, flag, start in ((outs[1], left_swap, 0), (outs[2], right_swap, rows - 2)):
                        one = res_s[0, f, i, start : start + 2]
                        two = res_s[1, f, i, start : start + 2]
                        ref[f, i, 0:2] = jnp.where(flag > 0, two, one)
                        ref[f, i, 2:4] = jnp.where(flag > 0, one, two)
        out_copies[-1].start()
        if final:
            out_copies[-2].start()

    base_at, u0, ready, done = 0, 0, 0, 0
    waited = False
    pending = []
    for r, length in enumerate(lengths):
        for t in range(length + 4):
            flag = None
            if plan["low_flag"] == r and t < 2:
                flag = 0
            if plan["high_flag"] == r and t >= length + 2:
                flag = 1
            flux(base_at + t, u0 + t - 2 if 2 <= t < length + 2 else None, flag)
            if t >= 4:
                finish(base_at + t - 2, u0 + t - 4)
                ready += 1
                if ready - done == GROUP or (ready == total and ready > done):
                    pending.append((done, ready - done))
                    done = ready
                    if len(pending) == 2:
                        if not waited:
                            wait_copies(weight_copies)
                            waited = True
                        multiply(*pending.pop(0))
        base_at += length + 4
        u0 += length
    if not waited:
        wait_copies(weight_copies)
    for item in pending:
        multiply(*item)
    if plan["tips"]:
        for target, start in ((outs[3], 0), (outs[4], total - 2)):
            tip = copy(res_s.at[:, :, start : start + 2], target)
            tip.start()
            out_copies.append(tip)
    wait_copies(out_copies)


def section_task(consts, factor, ranges, q_map, base_map, left_map, right_map, flags, planes, dims, name, final, tips):
    fields, rows, radii = dims
    arrays = {}

    def spans(kind, table, lists):
        held = arrays.setdefault(kind, [])
        out = []
        for planes_of_run in lists:
            sources = []
            for p in planes_of_run:
                array, at = table[p]
                index = next((i for i, a in enumerate(held) if a is array), None)
                if index is None:
                    index = len(held)
                    held.append(array)
                sources.append((index, at))
            out.append(merged(sources))
        return out

    wide = [list(range(a - 2, b + 2)) for a, b in ranges]
    tight = [list(range(a, b)) for a, b in ranges]
    mixed = base_map is not None
    plan = dict(
        dims=dims, lengths=[b - a for a, b in ranges], mixed=mixed, final=final, tips=tips,
        low_flag=next((i for i, r in enumerate(ranges) if r[0] == 0), None),
        high_flag=next((i for i, r in enumerate(ranges) if r[1] == planes), None),
        q=spans("q", q_map, wide), base=spans("base", base_map, tight) if mixed else [],
        left=spans("left", left_map, tight), right=spans("right", right_map, tight),
    )
    arrays.setdefault("base", [])
    plan["counts"] = [len(arrays[k]) for k in ("q", "base", "left", "right")]
    total = sum(plan["lengths"])
    spread = total + 4 * len(ranges)
    real = jax.ShapeDtypeStruct
    f32 = jnp.float32
    if final:
        out_shape = [real((fields, total, rows, radii), f32)] * 2
        out_specs = [anywhere] * 2
    else:
        out_shape = [real((2, fields, total, rows, radii), f32)] + [real((fields, total, 4, radii), f32)] * 2
        out_specs = [anywhere, vector, vector]
        if tips:
            out_shape += [real((2, fields, 2, rows, radii), f32)] * 2
            out_specs += [anywhere] * 2
    plan["outs"] = len(out_shape)
    copies = sum(len(s) for k in ("q", "base", "left", "right") for s in plan[k])
    copies += 2 + 2 * (total // GROUP + 2) + 2
    trig, edge_trig, radius, whi, wlo = consts
    operands = [flags, trig, edge_trig, radius, whi, wlo]
    operands += [a for k in ("q", "base", "left", "right") for a in arrays[k]]
    lines = fields * total * rows
    return pl.pallas_call(
        functools.partial(section_kernel, plan, factor),
        out_shape=out_shape,
        in_specs=[scalars, vector, vector, vector] + [anywhere] * (len(operands) - 4),
        out_specs=out_specs,
        scratch_shapes=[
            pltpu.VMEM((2, fields, spread, rows, radii), f32),
            pltpu.VMEM((2, fields, total, rows, radii) if mixed else (8, 128), f32),
            pltpu.VMEM((fields, total, 4, radii), f32),
            pltpu.VMEM((fields, total, 4, radii), f32),
            pltpu.VMEM(whi.shape, jnp.bfloat16),
            pltpu.VMEM(wlo.shape, jnp.bfloat16),
            pltpu.VMEM((2, fields, spread, rows, radii), f32),
            pltpu.VMEM((3, 2, fields, radii // 128, rows + 16, 128), f32),
            pltpu.VMEM((total, fields, rows, 4 * radii), jnp.bfloat16),
            pltpu.VMEM((total, fields, rows, 4 * radii), jnp.bfloat16),
            pltpu.VMEM((2, fields, total, rows, radii), f32),
            pltpu.SemaphoreType.DMA((copies,)),
        ],
        cost_estimate=pl.CostEstimate(
            flops=2 * lines * 4 * radii * 2 * radii * 6, bytes_accessed=8 * lines * radii * 4,
            transcendentals=0,
        ),
        name=name,
    )(*operands)


def gather_kernel(spans, tips, flags_ref, own_ref, even_ref, odd_ref, core_ref, *refs):
    outs, (q_s, sems) = refs[:-2], refs[-2:]
    _, fields, planes, rows, _ = q_s.shape
    c, keeps, h = flags_ref[5], flags_ref[6], flags_ref[3]
    far = q_s.at[1 - h]
    near = q_s.at[h]

    @pl.when(c == 0)
    def _():
        pltpu.make_async_copy(even_ref, far, sems.at[0]).start()

    @pl.when(c != 0)
    def _():
        pltpu.make_async_copy(odd_ref, far, sems.at[0]).start()

    @pl.when(keeps > 0)
    def _():
        lines = pl.ds(pl.multiple_of((1 - c) * rows, rows), rows)
        at = 0
        for i, (start, count) in enumerate(spans):
            pltpu.make_async_copy(
                own_ref.at[:, start : start + count, lines], near.at[:, at : at + count], sems.at[1 + i]
            ).start()
            at += count

    @pl.when(keeps == 0)
    def _():
        at = 0
        for i, (start, count) in enumerate(spans):
            pltpu.make_async_copy(
                core_ref.at[:, at : at + count], near.at[:, at : at + count], sems.at[1 + i]
            ).start()
            at += count

    pltpu.make_async_copy(even_ref, far, sems.at[0]).wait()
    at = 0
    for i, (start, count) in enumerate(spans):
        pltpu.make_async_copy(
            core_ref.at[:, at : at + count], near.at[:, at : at + count], sems.at[1 + i]
        ).wait()
        at += count
    last = 1 + len(spans)
    copies = [pltpu.make_async_copy(q_s, outs[0], sems.at[last])]
    if tips:
        copies.append(pltpu.make_async_copy(q_s.at[:, :, 0:2], outs[3], sems.at[last + 1]))
        copies.append(pltpu.make_async_copy(q_s.at[:, :, planes - 2 : planes], outs[4], sems.at[last + 2]))
    run_copies(copies)

    def edges(p, carry):
        for f in range(fields):
            for ref, flag, start in ((outs[1], flags_ref[2], 0), (outs[2], flags_ref[4], rows - 2)):
                one = q_s[0, f, p, start : start + 2]
                two = q_s[1, f, p, start : start + 2]
                ref[f, p, 0:2] = jnp.where(flag > 0, two, one)
                ref[f, p, 2:4] = jnp.where(flag > 0, one, two)
        return carry

    lax.fori_loop(0, planes, edges, 0)
    wait_copies(copies)


def gather_task(spans, tips, flags, own, even, odd, core, dims, name):
    fields, rows, radii = dims
    planes = sum(count for _, count in spans)
    f32 = jnp.float32
    out_shape = [jax.ShapeDtypeStruct((2, fields, planes, rows, radii), f32)]
    out_shape += [jax.ShapeDtypeStruct((fields, planes, 4, radii), f32)] * 2
    out_specs = [anywhere, vector, vector]
    if tips:
        out_shape += [jax.ShapeDtypeStruct((2, fields, 2, rows, radii), f32)] * 2
        out_specs += [anywhere] * 2
    return pl.pallas_call(
        functools.partial(gather_kernel, spans, tips),
        out_shape=out_shape,
        in_specs=[scalars] + [anywhere] * 4,
        out_specs=out_specs,
        scratch_shapes=[
            pltpu.VMEM((2, fields, planes, rows, radii), f32),
            pltpu.SemaphoreType.DMA((len(spans) + 4,)),
        ],
        cost_estimate=pl.CostEstimate(
            flops=0, bytes_accessed=16 * fields * planes * rows * radii, transcendentals=0
        ),
        name=name,
    )(flags, own, even, odd, core)


def place_kernel(spans, chained, flags_ref, near_ref, even_ref, odd_ref, core_ref, *refs):
    if chained:
        refs = refs[1:]
    out_ref, buf, sems = refs
    _, planes, both, _ = buf.shape
    rows = both // 2
    c, keeps = flags_ref[5], flags_ref[6]
    halves = [buf.at[:, :, :rows], buf.at[:, :, rows:]]

    def start(refs_of_halves):
        for e in range(2):
            pltpu.make_async_copy(refs_of_halves[e], halves[e], sems.at[e]).start()

    @pl.when(keeps == 0)
    def _():
        start([odd_ref, even_ref])

    @pl.when((keeps > 0) & (c == 0))
    def _():
        start([core_ref, near_ref])

    @pl.when((keeps > 0) & (c != 0))
    def _():
        start([near_ref, core_ref])

    for e in range(2):
        pltpu.make_async_copy(near_ref, halves[e], sems.at[e]).wait()
    copies, at = [], 0
    for i, (first, count) in enumerate(spans):
        copies.append(
            pltpu.make_async_copy(
                buf.at[:, at : at + count], out_ref.at[:, first : first + count], sems.at[2 + i]
            )
        )
        at += count
    run_copies(copies)
    wait_copies(copies)


def place_task(spans, flags, near, even, odd, core, whole, shape, name):
    fields, planes, ang_dev, radii = shape
    count = sum(n for _, n in spans)
    operands = [flags, near, even, odd, core] + ([] if whole is None else [whole])
    return pl.pallas_call(
        functools.partial(place_kernel, spans, whole is not None),
        out_shape=jax.ShapeDtypeStruct(shape, jnp.float32),
        in_specs=[scalars] + [anywhere] * (len(operands) - 1),
        out_specs=anywhere,
        scratch_shapes=[
            pltpu.VMEM((fields, count, ang_dev, radii), jnp.float32),
            pltpu.SemaphoreType.DMA((len(spans) + 2,)),
        ],
        input_output_aliases={} if whole is None else {5: 0},
        cost_estimate=pl.CostEstimate(
            flops=0, bytes_accessed=8 * fields * count * ang_dev * radii, transcendentals=0
        ),
        name=name,
    )(*operands)


def folded(matrix, radii):
    tall = jnp.concatenate([matrix[radii:], matrix[:radii][::-1]], axis=0)
    return jnp.concatenate([tall[:, radii:], tall[:, :radii][:, ::-1]], axis=1)


def per_device(conserved, deriv_matrix, filter_matrix):
    n = lax.axis_size("ang")
    count = lax.axis_size("ax")
    fields, planes, ang_dev, radii = conserved.shape
    rows = ang_dev // 2
    dims = (fields, rows, radii)
    half = n // 2
    total = ang_dev * n
    twist = total / (2.0 * math.pi * radii)
    pos = lax.axis_index("ang")
    layer = lax.axis_index("ax")
    h, j, c = pos // half, (pos % half) // 2, pos % 2
    ring = 4 * j + 2 * (h ^ (j & 1)) + 1 - c
    keeps = h == (c ^ (j & 1))

    def dev(hh, jj, cc):
        return hh * half + 2 * jj + cc

    spots = [(hh, jj, cc) for hh in range(2) for jj in range(n // 4) for cc in range(2)]
    givers = [(hh, jj, cc) for hh, jj, cc in spots if hh != (cc ^ (jj & 1))]
    keepers = [(hh, jj, cc) for hh, jj, cc in spots if hh == (cc ^ (jj & 1))]
    to_even = [(dev(*g), dev(1 - g[0], g[1], 0)) for g in givers]
    to_odd = [(dev(*g), dev(1 - g[0], g[1], 1)) for g in givers]
    to_core = [(dev(*k), dev(k[0], k[1], 1 - k[2])) for k in keepers]
    order = [dev((r % 4 // 2) ^ (r // 4 & 1), r // 4, 1 - r % 2) for r in range(n)]
    to_left = [(order[r], order[(r - 1) % n]) for r in range(n)]
    to_right = [(order[r], order[(r + 1) % n]) for r in range(n)]
    up = [(i, i + 1) for i in range(count - 1)]
    down = [(i + 1, i) for i in range(count - 1)]

    def back(table):
        return [(b, a) for a, b in table]

    flags = jnp.stack(
        [layer > 0, layer < count - 1, ring == 0, h == 1, ring == n - 1, c == 1, keeps]
    ).astype(jnp.int32)

    def angles(offsets):
        index = (ring * rows + offsets) % total
        return index.astype(jnp.float32) * (2.0 * math.pi / total)

    seg = jnp.arange(2, dtype=jnp.int32)[:, None] * (total // 2)
    centre = angles(seg + jnp.arange(rows, dtype=jnp.int32))
    left_rows = angles((seg + jnp.arange(-2, 0, dtype=jnp.int32)).reshape(4))
    right_rows = angles((seg + jnp.arange(rows, rows + 2, dtype=jnp.int32)).reshape(4))
    edges = jnp.stack([left_rows, right_rows])

    def spread(values):
        return jnp.broadcast_to(values[..., None], values.shape + (radii,))

    plain = jnp.stack([jnp.cos(centre), jnp.sin(centre)])
    plain_edges = jnp.stack([jnp.cos(edges), jnp.sin(edges)])
    radius = ((jnp.arange(radii, dtype=jnp.int32).astype(jnp.float32) + 0.5) / radii)[None]
    signs = jnp.where(jnp.arange(2 * radii, dtype=jnp.int32) < radii, -1.0, 1.0).astype(jnp.float32)

    outer = planes // 3
    span_outer = ((0, outer), (planes - outer, outer))
    span_inner = ((outer, planes - 2 * outer),)

    def cut(spans):
        parts = [lax.slice_in_dim(conserved, a, a + m, axis=1) for a, m in spans]
        block = parts[0] if len(parts) == 1 else jnp.concatenate(parts, axis=1)
        return block[:, :, :rows], block[:, :, rows:]

    def send(spans):
        first_half, second_half = cut(spans)
        odd = lax.ppermute(first_half, "ang", to_odd)
        even = lax.ppermute(second_half, "ang", to_even)
        core = lax.ppermute(jnp.where(c == 0, first_half, second_half), "ang", to_core)
        return even, odd, core

    def trade(left_edge, right_edge):
        return lax.ppermute(right_edge, "ang", to_right), lax.ppermute(left_edge, "ang", to_left)

    def trade_tips(low_tip, high_tip):
        return lax.ppermute(high_tip, "ax", up), lax.ppermute(low_tip, "ax", down)

    def listed(array, ranges):
        at, table = 0, {}
        for a, b in ranges:
            for p in range(a, b):
                table[p] = (array, at)
                at += 1
        return table

    def tipped(low, high):
        table = {p - 2: (low, p) for p in range(2)}
        table.update({planes + p: (high, p) for p in range(2)})
        return table

    sent_outer = send(span_outer)
    sent_inner = send(span_inner)

    composite = jnp.dot(filter_matrix, signs[:, None] * deriv_matrix, precision=highest)
    weights = jnp.concatenate([folded(filter_matrix, radii).T, folded(composite, radii).T], axis=0)
    whi, wlo = split_weights(weights)

    def consts(weight):
        scale = weight * courant * twist / 12.0
        return (
            spread(jnp.concatenate([plain, scale * plain])), spread(scale * plain_edges), radius, whi, wlo,
        )

    ro = ((0, outer), (planes - outer, planes))
    ri = ((outer, planes - outer),)
    one_o = ((0, outer - 2), (planes - outer + 2, planes))
    one_i = ((outer - 2, planes - outer + 2),)
    two_o = ((0, outer - 4), (planes - outer + 4, planes))
    two_i = ((outer - 4, planes - outer + 4),)

    def section(weight, ranges, maps, base_map, name, final=False, tips=False):
        q_map, left_map, right_map = maps
        return section_task(
            consts(weight), weight * courant, ranges, q_map, base_map, left_map, right_map,
            flags, planes, dims, name, final, tips,
        )

    q_o, left_o, right_o, low_tip, high_tip = gather_task(
        span_outer, True, flags, conserved, *sent_outer, dims, "gather_outer"
    )
    halo_left, halo_right = trade(left_o, right_o)
    low, high = trade_tips(low_tip, high_tip)
    q_map = {**listed(q_o, ro), **tipped(low, high)}
    lefts, rights = listed(halo_left, ro), listed(halo_right, ro)
    f_o, left_f, right_f, low_tip, high_tip = section(
        1.0, one_o, (q_map, lefts, rights), None, "section_one_outer", tips=True
    )
    low, high = trade_tips(low_tip, high_tip)
    f_map = {**listed(f_o, one_o), **tipped(low, high)}
    halo_left, halo_right = trade(left_f, right_f)
    f_lefts, f_rights = listed(halo_left, one_o), listed(halo_right, one_o)

    q_i, left_i, right_i = gather_task(
        span_inner, False, flags, conserved, *sent_inner, dims, "gather_inner"
    )
    halo_left, halo_right = trade(left_i, right_i)
    q_map.update(listed(q_i, ri))
    lefts.update(listed(halo_left, ri))
    rights.update(listed(halo_right, ri))

    near_o, far_o = section(
        0.5, two_o, (f_map, f_lefts, f_rights), q_map, "section_two_outer", final=True
    )

    def give_back(near, far):
        even = lax.ppermute(far, "ang", back(to_even))
        odd = lax.ppermute(far, "ang", back(to_odd))
        core = lax.ppermute(near, "ang", back(to_core))
        return even, odd, core

    back_o = give_back(near_o, far_o)

    f_i, left_f, right_f = section(1.0, one_i, (q_map, lefts, rights), None, "section_one_inner")
    halo_left, halo_right = trade(left_f, right_f)
    f_map.update(listed(f_i, one_i))
    f_lefts.update(listed(halo_left, one_i))
    f_rights.update(listed(halo_right, one_i))
    near_i, far_i = section(
        0.5, two_i, (f_map, f_lefts, f_rights), q_map, "section_two_inner", final=True
    )
    back_i = give_back(near_i, far_i)

    def spans_of(ranges):
        return tuple((a, b - a) for a, b in ranges)

    out = place_task(spans_of(two_o), flags, near_o, *back_o, None, conserved.shape, "place_outer")
    return place_task(spans_of(two_i), flags, near_i, *back_i, out, conserved.shape, "place_inner")


def solution(mesh):
    placed = (P(None, "ax", "ang", None), P(), P())
    return jax.shard_map(
        per_device,
        mesh=mesh,
        in_specs=placed,
        out_specs=P(None, "ax", "ang", None),
        check_vma=False,
    )
```

```python
import functools
import math

import jax
import jax.numpy as jnp
from jax import lax
from jax.experimental import pallas as pl
from jax.experimental.pallas import tpu as pltpu
from jax.sharding import PartitionSpec as P


gamma_ratio = 1.4
courant = 0.15
anywhere = pl.BlockSpec(memory_space=pl.ANY)
scalars = pl.BlockSpec(memory_space=pltpu.SMEM)
vector = pl.BlockSpec(memory_space=pltpu.VMEM)
GROUP = 4
TAILS = 2


def ready(flags, *early):
    def copy_flags(flags_ref, *refs):
        for i in range(flags_ref.shape[0]):
            refs[-1][i] = flags_ref[i]

    return pl.pallas_call(
        copy_flags, out_shape=jax.ShapeDtypeStruct(flags.shape, flags.dtype),
        in_specs=[scalars] + [anywhere] * len(early), out_specs=scalars, name="ready",
    )(flags, *early)


def split_weights(w):
    high = lax.reduce_precision(w, 8, 7)
    return high.astype(jnp.bfloat16), (w - high).astype(jnp.bfloat16)


_, _, SWAP_LEFT, SWAP_RIGHT, SEG, ODD, HALF = range(7)


def speeds(q):
    rho, mx, my, mz, en = q
    inv = 1.0 / rho
    ux, uy, uz = mx * inv, my * inv, mz * inv
    pressure = (gamma_ratio - 1.0) * (en - 0.5 * (mx * ux + my * uy + mz * uz))
    return ux, uy, uz, pressure, en + pressure


def angular_of(q, state, cos, sin):
    rho, mx, my, mz, _ = q
    ux, uy, _, pressure, enthalpy = state
    us = uy * cos - ux * sin
    return (rho * us, mx * us - pressure * sin, my * us + pressure * cos, mz * us, enthalpy * us)


def radial_of(q, state, cos, sin, scale):
    rho, mx, my, mz, _ = q
    ux, uy, _, pressure, enthalpy = state
    ur = (ux * cos + uy * sin) * scale
    ps = pressure * scale
    return (rho * ur, mx * ur + ps * cos, my * ur + ps * sin, mz * ur, enthalpy * ur)


def axial_of(q, state, scale):
    _, mx, my, mz, _ = q
    _, _, uz, pressure, enthalpy = state
    uz = uz * scale
    return (mz * scale, mx * uz, my * uz, mz * uz + pressure * scale, enthalpy * uz)


def run_copies(copies):
    for copy in copies:
        copy.start()


def wait_copies(copies):
    for copy in copies:
        copy.wait()


def section_kernel(plan, factor, *refs):
    fields, rows, radii = plan["dims"]
    lengths, mixed, final = plan["lengths"], plan["mixed"], plan["final"]
    total = sum(lengths)
    counts = plan["counts"]
    refs = list(refs)
    flags_ref, table_ref, radius_ref, whi_hbm, wlo_hbm = refs[:5]
    del refs[:5]
    groups = []
    for count in counts:
        groups.append(refs[:count])
        del refs[:count]
    q_in, tip_in, base_in, left_in, right_in = groups
    outs = refs[: plan["outs"]]
    del refs[: plan["outs"]]
    q_s, base_s, whi_s, wlo_s, axial_s, ang_s, hi_s, lo_s, res_s, sems = refs
    lane_halves = radii // 128

    used = [0]

    def copy(src, dst):
        used[0] += 1
        return pltpu.make_async_copy(src, dst, sems.at[used[0] - 1])

    seg = flags_ref[SEG]

    def table(k, s):
        row = plan["table"] + (2 * k + s) * rows
        return jnp.concatenate([table_ref[row : row + rows]] * lane_halves, axis=1)

    def edge_table(k, side):
        row = plan["table"] + 8 * rows + (2 * k + side) * 8
        return jnp.concatenate([table_ref[row : row + 4]] * lane_halves, axis=1)

    loads, q_wait, base_wait = [], {}, {}

    def load(source, target, start, at, size):
        if len(source) == 1:
            return [copy(source[0].at[:, :, start : start + size], target.at[:, :, at : at + size])]
        return [
            copy(source[0].at[:, start : start + size], target.at[seg, :, at : at + size]),
            copy(source[1].at[:, start : start + size], target.at[1 - seg, :, at : at + size]),
        ]

    def sources(kind, held):
        held, out = list(held), []
        for width in plan["widths"][kind]:
            out.append(held[:width])
            del held[:width]
        return out

    q_from, base_from = sources("q", q_in), sources("base", base_in)
    for array, start, at, size in plan["q"]:
        q_wait[at] = load(q_from[array], q_s, start, at, size)
        loads += [(at, one) for one in q_wait[at]]
    if mixed:
        for array, start, at, size in plan["base"]:
            base_wait[at] = load(base_from[array], base_s, start, at, size)
            loads += [(at + 4, one) for one in base_wait[at]]
    weight_copies = [copy(whi_hbm, whi_s), copy(wlo_hbm, wlo_s)]
    loads += [(9, one) for one in weight_copies]
    run_copies([one for _, one in sorted(loads, key=lambda item: item[0])])

    axial_scale = (factor / 12.0) * radius_ref[...]
    radial_scale = -factor * radius_ref[...]

    def put(u, f, column, value):
        lanes = slice(column, column + value.shape[-1])
        hi = value.astype(jnp.bfloat16)
        hi_s[u, f, :, lanes] = hi
        lo_s[u, f, :, lanes] = (value - hi.astype(jnp.float32)).astype(jnp.bfloat16)

    def flux(at, u, flag):
        inner = u is not None
        tip = plan["tip"].get(at)
        if at in q_wait:
            wait_copies(q_wait[at])
        if inner:
            slot = u % 3
            edge = []
            for side, (array, start) in ((0, plan["left"][u]), (1, plan["right"][u])):
                ref = (left_in, right_in)[side][array]
                q = tuple(ref[f, start] for f in range(fields))
                edge.append(angular_of(q, speeds(q), edge_table(0, side), edge_table(1, side)))
        for s in range(2):
            if tip is None:
                q = tuple(q_s[s, f, at] for f in range(fields))
            else:
                swap_tip, other_tip = (tip_in[0], tip_in[1]) if tip[0] == "high" else (tip_in[1], tip_in[0])
                q = tuple(
                    jnp.where(flags_ref[ODD] > 0, other_tip[s, f, tip[1]], swap_tip[s, f, tip[1]])
                    for f in range(fields)
                )
            state = speeds(q)
            axial = axial_of(q, state, axial_scale)
            for f in range(fields):
                value = axial[f]
                if flag is not None:
                    value = jnp.where(flags_ref[flag] > 0, value, 0.0)
                axial_s[s, f, at] = value
            if not inner:
                continue
            radial = radial_of(q, state, table(0, s), table(1, s), radial_scale)
            for f in range(fields):
                put(u, f, 2 * radii + s * radii, radial[f])
            angular = angular_of(q, state, table(2, s), table(3, s))
            for f in range(fields):
                for l in range(lane_halves):
                    lanes = slice(l * 128, l * 128 + 128)
                    ang_s[slot, s, f, l, 8 : 8 + rows] = angular[f][:, lanes]
                    ang_s[slot, s, f, l, 6:8] = edge[0][f][2 * s : 2 * s + 2, lanes]
                    ang_s[slot, s, f, l, 8 + rows : 10 + rows] = edge[1][f][2 * s : 2 * s + 2, lanes]

    def finish(at, u):
        slot = u % 3
        if u in base_wait:
            wait_copies(base_wait[u])
        for s in range(2):
            for f in range(fields):
                for l in range(lane_halves):
                    lanes = slice(l * 128, l * 128 + 128)

                    def ang(k):
                        return ang_s[slot, s, f, l, 8 + k : 8 + k + rows]

                    def axi(k):
                        return axial_s[s, f, at + k, :, lanes]

                    near = (ang(1) - ang(-1)) + (axi(1) - axi(-1))
                    far = (ang(2) - ang(-2)) + (axi(2) - axi(-2))
                    own = q_s[s, f, at, :, lanes]
                    if mixed:
                        own = 0.5 * base_s[s, f, u, :, lanes] + 0.5 * own
                    put(u, f, s * radii + l * 128, (own - 8.0 * near) + far)

    left_swap, right_swap = flags_ref[SWAP_LEFT], flags_ref[SWAP_RIGHT]
    out_copies = []

    def multiply(first, count):
        hi = hi_s[first : first + count].reshape(count * fields * rows, 4 * radii)
        lo = lo_s[first : first + count].reshape(count * fields * rows, 4 * radii)
        dot = functools.partial(jnp.dot, preferred_element_type=jnp.float32)
        for s in range(2):
            columns = slice(s * radii, s * radii + radii)
            whi = whi_s[:, columns]
            res = dot(hi, whi) + dot(lo, whi) + dot(hi, wlo_s[:, columns])
            where = jnp.bitwise_xor(seg, s) if final else s
            for i in range(count):
                for f in range(fields):
                    start = (i * fields + f) * rows
                    res_s[where, f, first + i] = res[start : start + rows]
        if final:
            pieces = [(res_s.at[0], outs[0]), (res_s.at[1], outs[1])]
            for source, target in pieces:
                out_copies.append(
                    copy(source.at[:, first : first + count], target.at[:, first : first + count])
                )
        else:
            out_copies.append(
                copy(res_s.at[:, :, first : first + count], outs[0].at[:, :, first : first + count])
            )
            for i in range(first, first + count):
                for f in range(fields):
                    for ref, flag, start in ((outs[1], left_swap, 0), (outs[2], right_swap, rows - 2)):
                        one = res_s[0, f, i, start : start + 2]
                        two = res_s[1, f, i, start : start + 2]
                        ref[f, i, 0:2] = jnp.where(flag > 0, two, one)
                        ref[f, i, 2:4] = jnp.where(flag > 0, one, two)
        out_copies[-1].start()
        if final:
            out_copies[-2].start()

    base_at, u0, ready, done = 0, 0, 0, 0
    waited = False
    pending = []
    for r, length in enumerate(lengths):
        for t in range(length + 4):
            flag = None
            if plan["low_flag"] == r and t < 2:
                flag = 0
            if plan["high_flag"] == r and t >= length + 2:
                flag = 1
            flux(base_at + t, u0 + t - 2 if 2 <= t < length + 2 else None, flag)
            if t >= 4:
                finish(base_at + t - 2, u0 + t - 4)
                ready += 1
                if ready - done == GROUP or (ready == total and ready > done):
                    pending.append((done, ready - done))
                    done = ready
                    if len(pending) == 2:
                        if not waited:
                            wait_copies(weight_copies)
                            waited = True
                        multiply(*pending.pop(0))
        base_at += length + 4
        u0 += length
    if not waited:
        wait_copies(weight_copies)
    for item in pending:
        multiply(*item)
    if plan["tips"]:
        last = jnp.where(flags_ref[ODD] > 0, 0, total - 2)
        for target, start in ((outs[3], last), (outs[4], total - 2 - last)):
            tip = copy(res_s.at[:, :, pl.ds(start, 2)], target)
            tip.start()
            out_copies.append(tip)
    wait_copies(out_copies)


def section_task(consts, factor, ranges, q_map, base_map, left_map, right_map, flags, planes, dims, final, tips):
    fields, rows, radii = dims
    arrays = {kind: [] for kind in ("q", "tip", "base", "left", "right")}

    def index_of(kind, array):
        held = arrays[kind]
        if not any(a is array for a in held):
            held.append(array)
        return next(i for i, a in enumerate(held) if a is array)

    def flat(kind):
        return [one for a in arrays[kind] for one in (a if isinstance(a, tuple) else (a,))]

    def pieces(kind, table, wanted):
        spans = []
        for at, p in enumerate(wanted):
            array, start = table[p]
            index = index_of(kind, array)
            last = spans[-1] if spans else None
            if last and last[0] == index and last[1] + last[3] == start and last[2] + last[3] == at and last[3] < GROUP:
                last[3] += 1
            else:
                spans.append([index, start, at, 1])
        return spans

    table_row = consts[1]
    wide = [p for a, b in ranges for p in range(a - 2, b + 2)]
    tight = [p for a, b in ranges for p in range(a, b)]
    mixed = base_map is not None
    tips_at = {at: p for at, p in enumerate(wide) if p < 0 or p >= planes}
    kept = [(at, p) for at, p in enumerate(wide) if at not in tips_at]
    q_spans = pieces("q", q_map, [p for _, p in kept])
    q_spans = [[i, start, kept[at][0], size] for i, start, at, size in q_spans]
    plan = dict(
        dims=dims, lengths=[b - a for a, b in ranges], mixed=mixed, final=final, tips=tips,
        low_flag=next((i for i, r in enumerate(ranges) if r[0] == 0), None),
        high_flag=next((i for i, r in enumerate(ranges) if r[1] == planes), None),
        q=q_spans, tip={at: ("low" if p < 0 else "high", p + 2 if p < 0 else p - planes) for at, p in tips_at.items()},
        table=table_row,
        base=pieces("base", base_map, tight) if mixed else [],
        left=[(index_of("left", left_map[p][0]), left_map[p][1]) for p in tight],
        right=[(index_of("right", right_map[p][0]), right_map[p][1]) for p in tight],
    )
    kinds = ("q", "tip", "base", "left", "right")
    if tips_at:
        arrays["tip"] = list(q_map["tips"])
    plan["counts"] = [len(flat(k)) for k in kinds]
    plan["widths"] = {k: [len(a) if isinstance(a, tuple) else 1 for a in arrays[k]] for k in ("q", "base")}
    total = sum(plan["lengths"])
    spread = total + 4 * len(ranges)
    real = jax.ShapeDtypeStruct
    f32 = jnp.float32
    if final:
        out_shape = [real((fields, total, rows, radii), f32)] * 2
        out_specs = [anywhere] * 2
    else:
        out_shape = [real((2, fields, total, rows, radii), f32)] + [real((fields, total, 4, radii), f32)] * 2
        out_specs = [anywhere, vector, vector]
        if tips:
            out_shape += [real((2, fields, 2, rows, radii), f32)] * 2
            out_specs += [anywhere] * 2
    plan["outs"] = len(out_shape)
    copies = 2 * len(plan["q"]) + 2 * len(plan["base"]) + 2 + 2 * (total // GROUP + 2) + 2
    table, table_row, radius, whi, wlo = consts
    operands = [flags, table, radius, whi, wlo]
    operands += [a for k in kinds for a in flat(k)]
    places = [scalars, vector, vector, anywhere, anywhere]
    places += [vector if k in ("tip", "left", "right") else anywhere for k in kinds for _ in flat(k)]
    lines = fields * total * rows
    return pl.pallas_call(
        functools.partial(section_kernel, plan, factor),
        out_shape=out_shape,
        in_specs=places,
        out_specs=out_specs,
        scratch_shapes=[
            pltpu.VMEM((2, fields, spread, rows, radii), f32),
            pltpu.VMEM((2, fields, total, rows, radii) if mixed else (8, 128), f32),
            pltpu.VMEM(whi.shape, jnp.bfloat16),
            pltpu.VMEM(wlo.shape, jnp.bfloat16),
            pltpu.VMEM((2, fields, spread, rows, radii), f32),
            pltpu.VMEM((3, 2, fields, radii // 128, rows + 16, 128), f32),
            pltpu.VMEM((total, fields, rows, 4 * radii), jnp.bfloat16),
            pltpu.VMEM((total, fields, rows, 4 * radii), jnp.bfloat16),
            pltpu.VMEM((2, fields, total, rows, radii), f32),
            pltpu.SemaphoreType.DMA((copies,)),
        ],
        cost_estimate=pl.CostEstimate(
            flops=2 * lines * 4 * radii * 2 * radii * 6, bytes_accessed=8 * lines * radii * 4,
            transcendentals=0,
        ),
    )(*operands)


def parts_of(spans):
    parts, at = [], 0
    for start, count in spans:
        for i in range(0, count, GROUP):
            size = min(GROUP, count - i)
            parts.append((start + i, at + i, size))
        at += count
    return parts


def edges_kernel(tips, flags_ref, one_ref, two_ref, *refs):
    outs, (q_s, sems) = refs[:-2], refs[-2:]
    _, fields, planes, rows, _ = q_s.shape
    seg = flags_ref[SEG]
    parts = parts_of(((0, planes),))
    loads = []
    for i, (_, at, size) in enumerate(parts):
        span = slice(at, at + size)
        loads.append(
            [
                pltpu.make_async_copy(one_ref.at[:, span], q_s.at[seg, :, span], sems.at[2 * i]),
                pltpu.make_async_copy(two_ref.at[:, span], q_s.at[1 - seg, :, span], sems.at[2 * i + 1]),
            ]
        )
        run_copies(loads[-1])

    def edges(p, carry):
        for f in range(fields):
            for ref, flag, start in (
                (outs[0], flags_ref[SWAP_LEFT], 0), (outs[1], flags_ref[SWAP_RIGHT], rows - 2)
            ):
                one = q_s[0, f, p, start : start + 2]
                two = q_s[1, f, p, start : start + 2]
                ref[f, p, 0:2] = jnp.where(flag > 0, two, one)
                ref[f, p, 2:4] = jnp.where(flag > 0, one, two)
        return carry

    for i, (_, at, size) in enumerate(parts):
        wait_copies(loads[i])
        lax.fori_loop(at, at + size, edges, 0)
    if tips:
        last = jnp.where(flags_ref[ODD] > 0, 0, planes - 2)
        copies = [
            pltpu.make_async_copy(
                q_s.at[:, :, pl.ds(start, 2)], outs[2 + i], sems.at[2 * len(parts) + i]
            )
            for i, start in enumerate((last, planes - 2 - last))
        ]
        run_copies(copies)
        wait_copies(copies)


def edges_task(tips, flags, one, two, dims):
    fields, rows, radii = dims
    planes = one.shape[1]
    f32 = jnp.float32
    out_shape = [jax.ShapeDtypeStruct((fields, planes, 4, radii), f32)] * 2
    out_specs = [vector, vector]
    if tips:
        out_shape += [jax.ShapeDtypeStruct((2, fields, 2, rows, radii), f32)] * 2
        out_specs += [anywhere] * 2
    return pl.pallas_call(
        functools.partial(edges_kernel, tips),
        out_shape=out_shape,
        in_specs=[scalars] + [anywhere] * 2,
        out_specs=out_specs,
        scratch_shapes=[
            pltpu.VMEM((2, fields, planes, rows, radii), f32),
            pltpu.SemaphoreType.DMA((2 * len(parts_of(((0, planes),))) + 2,)),
        ],
        cost_estimate=pl.CostEstimate(
            flops=0, bytes_accessed=8 * fields * planes * rows * radii, transcendentals=0
        ),
    )(flags, one, two)


def place_kernel(spans, chained, flags_ref, one_ref, two_ref, *refs):
    if chained:
        refs = refs[1:]
    out_ref, buf, sems = refs
    rows = buf.shape[2] // 2
    half = flags_ref[HALF]
    parts = parts_of(spans)
    loads = []
    for i, (_, at, size) in enumerate(parts):
        span = slice(at, at + size)
        loads.append(
            [
                pltpu.make_async_copy(
                    ref.at[:, span],
                    buf.at[:, span, pl.ds(pl.multiple_of(row * rows, rows), rows)], sems.at[2 * i + e],
                )
                for e, (ref, row) in enumerate(((one_ref, half), (two_ref, 1 - half)))
            ]
        )
        run_copies(loads[-1])
    copies = []
    for i, (first, at, size) in enumerate(parts):
        wait_copies(loads[i])
        one = pltpu.make_async_copy(
            buf.at[:, at : at + size], out_ref.at[:, first : first + size], sems.at[2 * len(parts) + i]
        )
        one.start()
        copies.append(one)
    wait_copies(copies)


def place_task(spans, flags, one, two, whole, shape):
    fields, _, ang_dev, radii = shape
    count = sum(n for _, n in spans)
    operands = [flags, one, two] + ([] if whole is None else [whole])
    return pl.pallas_call(
        functools.partial(place_kernel, spans, whole is not None),
        out_shape=jax.ShapeDtypeStruct(shape, jnp.float32),
        in_specs=[scalars] + [anywhere] * (len(operands) - 1),
        out_specs=anywhere,
        scratch_shapes=[
            pltpu.VMEM((fields, count, ang_dev, radii), jnp.float32),
            pltpu.SemaphoreType.DMA((3 * len(parts_of(spans)),)),
        ],
        input_output_aliases={} if whole is None else {3: 0},
        cost_estimate=pl.CostEstimate(
            flops=0, bytes_accessed=8 * fields * count * ang_dev * radii, transcendentals=0
        ),
    )(*operands)


def folded(matrix, radii):
    tall = jnp.concatenate([matrix[radii:], matrix[:radii][::-1]], axis=0)
    return jnp.concatenate([tall[:, radii:], tall[:, :radii][:, ::-1]], axis=1)


def per_device(conserved, deriv_matrix, filter_matrix):
    n = lax.axis_size("ang")
    count = lax.axis_size("ax")
    fields, planes, ang_dev, radii = conserved.shape
    rows = ang_dev // 2
    dims = (fields, rows, radii)
    half = n // 2
    total = ang_dev * n
    twist = total / (2.0 * math.pi * radii)
    pos = lax.axis_index("ang")
    layer = lax.axis_index("ax")
    h, j, c = pos // half, (pos % half) // 2, pos % 2
    ring = 4 * j + 2 * (h ^ (j & 1)) + 1 - c
    keeps = h == (c ^ (j & 1))

    def dev(hh, jj, cc):
        return hh * half + 2 * jj + cc

    cycle, swap = [], []
    for jj in range(n // 4):
        odd = jj & 1
        keeper = [dev(hh, jj, hh ^ odd) for hh in range(2)]
        giver = [dev(hh, jj, 1 - (hh ^ odd)) for hh in range(2)]
        ring_of_four = [giver[0], keeper[1], giver[1], keeper[0]]
        cycle += [(ring_of_four[i], ring_of_four[(i + 1) % 4]) for i in range(4)]
        swap += [(giver[0], giver[1]), (giver[1], giver[0]), (keeper[0], keeper[0]), (keeper[1], keeper[1])]
    order = [dev((r % 4 // 2) ^ (r // 4 & 1), r // 4, 1 - r % 2) for r in range(n)]
    to_left = [(order[r], order[(r - 1) % n]) for r in range(n)]
    to_right = [(order[r], order[(r + 1) % n]) for r in range(n)]

    def layer_swap(first):
        table = {i: i for i in range(count)}
        for i in range(first, count - 1, 2):
            table[i], table[i + 1] = i + 1, i
        return sorted(table.items())

    def back(table):
        return [(b, a) for a, b in table]

    sent_half = h ^ (j & 1)
    flags = jnp.stack(
        [layer > 0, layer < count - 1, ring == 0, ring == n - 1, (h == 1) ^ keeps, layer % 2 == 1, sent_half == 1]
    ).astype(jnp.int32)

    def angles(offsets):
        index = (ring * rows + offsets) % total
        return index.astype(jnp.float32) * (2.0 * math.pi / total)

    seg = jnp.arange(2, dtype=jnp.int32)[:, None] * (total // 2)
    centre = angles(seg + jnp.arange(rows, dtype=jnp.int32))
    left_rows = angles((seg + jnp.arange(-2, 0, dtype=jnp.int32)).reshape(4))
    right_rows = angles((seg + jnp.arange(rows, rows + 2, dtype=jnp.int32)).reshape(4))
    edges = jnp.stack([left_rows, right_rows])

    def trig_rows(weight):
        scale = weight * courant * twist / 12.0
        inner = jnp.stack([jnp.cos(centre), jnp.sin(centre)])
        outer_rows = jnp.pad(scale * jnp.stack([jnp.cos(edges), jnp.sin(edges)]), ((0, 0), (0, 0), (0, 4)))
        return jnp.concatenate([inner.reshape(-1), (scale * inner).reshape(-1), outer_rows.reshape(-1)])

    trig_values = jnp.concatenate([trig_rows(1.0), trig_rows(0.5)])
    table = jnp.broadcast_to(trig_values[:, None], (trig_values.shape[0], 128))
    radius = ((jnp.arange(radii, dtype=jnp.int32).astype(jnp.float32) + 0.5) / radii)[None]
    signs = jnp.where(jnp.arange(2 * radii, dtype=jnp.int32) < radii, -1.0, 1.0).astype(jnp.float32)

    outer = planes // 3
    span_outer = ((0, outer), (planes - outer, outer))
    span_inner = ((outer, planes - 2 * outer),)

    def cut(spans):
        parts = [lax.slice_in_dim(conserved, a, a + m, axis=1) for a, m in spans]
        block = parts[0] if len(parts) == 1 else jnp.concatenate(parts, axis=1)
        return block[:, :, :rows], block[:, :, rows:]

    def send(spans):
        first_half, second_half = cut(spans)
        one = jnp.where(sent_half == 0, first_half, second_half)
        two = jnp.where(sent_half == 0, second_half, first_half)
        return lax.ppermute(one, "ang", cycle), lax.ppermute(two, "ang", swap)

    def trade(left_edge, right_edge):
        left = lax.ppermute(right_edge, "ang", to_right)
        return left, lax.ppermute(left_edge, "ang", to_left)

    def trade_tips(one, two):
        one = lax.ppermute(one, "ax", layer_swap(0))
        return one, lax.ppermute(two, "ax", layer_swap(1))

    def listed(array, ranges):
        at, table = 0, {}
        for a, b in ranges:
            for p in range(a, b):
                table[p] = (array, at)
                at += 1
        return table

    sent_outer = send(span_outer)
    sent_inner = send(span_inner)

    composite = jnp.dot(filter_matrix, signs[:, None] * deriv_matrix, precision=lax.Precision.HIGH)
    weights = jnp.concatenate([folded(filter_matrix, radii).T, folded(composite, radii).T], axis=0)

    whi, wlo = split_weights(weights)
    flags = ready(flags, whi, wlo, table, radius)

    ro = ((0, outer), (planes - outer, planes))
    ri = ((outer, planes - outer),)
    one_o = ((0, outer - 2), (planes - outer + 2, planes))
    one_i = ((outer - 2, planes - outer + 2),)
    two_o = ((0, outer - 4), (planes - outer + 4, planes))
    cuts = [outer - 4 + (planes - 2 * outer + 8) * i // TAILS for i in range(TAILS + 1)]

    def section(weight, ranges, maps, base_map, final=False, tips=False):
        q_map, left_map, right_map = maps
        return section_task(
            (table, 0 if weight == 1.0 else trig_values.shape[0] // 2, radius, whi, wlo), weight * courant, ranges, q_map, base_map, left_map,
            right_map, flags, planes, dims, final, tips,
        )

    left_o, right_o, tip_one, tip_two = edges_task(True, flags, *sent_outer, dims)
    halo_left, halo_right = trade(left_o, right_o)
    q_map = listed(sent_outer, ro)
    q_map["tips"] = trade_tips(tip_one, tip_two)
    lefts, rights = listed(halo_left, ro), listed(halo_right, ro)
    f_o, left_f, right_f, tip_one, tip_two = section(1.0, one_o, (q_map, lefts, rights), None, tips=True)
    halo_left, halo_right = trade(left_f, right_f)
    f_map = listed(f_o, one_o)
    f_map["tips"] = trade_tips(tip_one, tip_two)
    f_lefts, f_rights = listed(halo_left, one_o), listed(halo_right, one_o)

    left_i, right_i = edges_task(False, flags, *sent_inner, dims)
    halo_left, halo_right = trade(left_i, right_i)
    q_map.update(listed(sent_inner, ri))
    lefts.update(listed(halo_left, ri))
    rights.update(listed(halo_right, ri))

    def give_back(one, two):
        one = lax.ppermute(one, "ang", back(cycle))
        return one, lax.ppermute(two, "ang", back(swap))

    backs = []
    near, far = section(0.5, two_o, (f_map, f_lefts, f_rights), q_map, final=True)
    backs.append((two_o, give_back(near, far)))

    f_i, left_f, right_f = section(1.0, one_i, (q_map, lefts, rights), None)
    halo_left, halo_right = trade(left_f, right_f)
    f_map.update(listed(f_i, one_i))
    f_lefts.update(listed(halo_left, one_i))
    f_rights.update(listed(halo_right, one_i))
    for i in range(TAILS):
        ranges = ((cuts[i], cuts[i + 1]),)
        near, far = section(0.5, ranges, (f_map, f_lefts, f_rights), q_map, final=True)
        backs.append((ranges, give_back(near, far)))

    out = None
    for ranges, arrived in backs:
        spans = tuple((a, b - a) for a, b in ranges)
        out = place_task(spans, flags, *arrived, out, conserved.shape)
    return out


def solution(mesh):
    placed = (P(None, "ax", "ang", None), P(), P())

    return jax.shard_map(
        per_device,
        mesh=mesh,
        in_specs=placed,
        out_specs=P(None, "ax", "ang", None),
        check_vma=False,
    )
```

```python
import functools
import math

import jax
import jax.numpy as jnp
from jax import lax
from jax.experimental import pallas as pl
from jax.experimental.pallas import tpu as pltpu
from jax.sharding import PartitionSpec as P


gamma_ratio = 1.4
courant = 0.15
anywhere = pl.BlockSpec(memory_space=pl.ANY)
scalars = pl.BlockSpec(memory_space=pltpu.SMEM)
vector = pl.BlockSpec(memory_space=pltpu.VMEM)
GROUP = 4
TAILS = 2
OUTER = 8
SECTION_VMEM = 28 << 20
COPY_VMEM = 8 << 20


def prepare_kernel(flags_ref, filter_ref, deriv_ref, table_ref, radius_ref, flags_out, hi_ref, lo_ref):
    for i in range(flags_ref.shape[0]):
        flags_out[i] = flags_ref[i]
    size = filter_ref.shape[0]
    half = size // 2
    dot = functools.partial(jnp.dot, preferred_element_type=jnp.float32)

    def fold(flip):
        row = lax.broadcasted_iota(jnp.int32, (size, size), flip)
        column = lax.broadcasted_iota(jnp.int32, (size, size), 1 - flip)
        return (column == jnp.where(row < half, row + half, size - 1 - row)).astype(jnp.bfloat16)

    into, back_out = fold(0), fold(1)

    def split(value):
        hi = value.astype(jnp.bfloat16)
        return hi, (value - hi.astype(jnp.float32)).astype(jnp.bfloat16)

    def folded(matrix):
        turned = lax.dot_general(
            into, matrix, (((1,), (1,)), ((), ())), preferred_element_type=jnp.float32
        ).astype(jnp.bfloat16)
        return dot(turned, back_out)

    filter_hi, filter_lo = (folded(part) for part in split(filter_ref[...]))
    deriv_hi, deriv_lo = (folded(part).astype(jnp.bfloat16) for part in split(deriv_ref[...]))
    hi_ref[:size] = filter_hi.astype(jnp.bfloat16)
    lo_ref[:size] = filter_lo.astype(jnp.bfloat16)
    row = lax.broadcasted_iota(jnp.int32, (size, size), 0)
    sign = jnp.where(row < half, 1.0, -1.0)
    signed_hi = (sign * filter_hi).astype(jnp.bfloat16)
    signed_lo = (sign * filter_lo).astype(jnp.bfloat16)
    both = dot(deriv_hi, signed_hi) + dot(deriv_lo, signed_hi) + dot(deriv_hi, signed_lo)
    hi, lo = split(both)
    hi_ref[size:] = hi
    lo_ref[size:] = lo


def prepare(flags, filter_matrix, deriv_matrix, table, radius):
    size = filter_matrix.shape[0]
    half = jax.ShapeDtypeStruct((2 * size, size), jnp.bfloat16)
    return pl.pallas_call(
        prepare_kernel,
        out_shape=(jax.ShapeDtypeStruct(flags.shape, flags.dtype), half, half),
        in_specs=[scalars, vector, vector, anywhere, anywhere],
        out_specs=(scalars, vector, vector),
        compiler_params=pltpu.CompilerParams(vmem_limit_bytes=3 * COPY_VMEM),
        name="prepare",
    )(flags, filter_matrix, deriv_matrix, table, radius)


def cut_kernel(spans, flags_ref, own_ref, out_ref, sems):
    rows = out_ref.shape[2]
    half = 1 - flags_ref[HALF]
    copies = []
    for i, (start, at, size) in enumerate(parts_of(spans)):
        copies.append(
            pltpu.make_async_copy(
                own_ref.at[:, start : start + size, pl.ds(pl.multiple_of(half * rows, rows), rows)],
                out_ref.at[:, at : at + size], sems.at[i],
            )
        )
    run_copies(copies)
    wait_copies(copies)


def cut_task(spans, flags, own):
    fields, _, both, radii = own.shape
    planes = sum(count for _, count in spans)
    return pl.pallas_call(
        functools.partial(cut_kernel, spans),
        out_shape=jax.ShapeDtypeStruct((fields, planes, both // 2, radii), own.dtype),
        in_specs=[scalars, pl.BlockSpec(memory_space=pltpu.HBM)], out_specs=vector,
        scratch_shapes=[pltpu.SemaphoreType.DMA((len(parts_of(spans)),))],
        compiler_params=pltpu.CompilerParams(vmem_limit_bytes=COPY_VMEM),
        cost_estimate=pl.CostEstimate(
            flops=0, bytes_accessed=4 * fields * planes * both * radii, transcendentals=0
        ),
    )(flags, own)


_, _, SWAP_LEFT, SWAP_RIGHT, SEG, ODD, HALF = range(7)


def speeds(q):
    rho, mx, my, mz, en = q
    inv = 1.0 / rho
    ux, uy, uz = mx * inv, my * inv, mz * inv
    pressure = (gamma_ratio - 1.0) * (en - 0.5 * (mx * ux + my * uy + mz * uz))
    return ux, uy, uz, pressure, en + pressure


def angular_of(q, state, cos, sin):
    rho, mx, my, mz, _ = q
    ux, uy, _, pressure, enthalpy = state
    us = uy * cos - ux * sin
    return (rho * us, mx * us - pressure * sin, my * us + pressure * cos, mz * us, enthalpy * us)


def radial_of(q, state, cos, sin, scale):
    rho, mx, my, mz, _ = q
    ux, uy, _, pressure, enthalpy = state
    ur = (ux * cos + uy * sin) * scale
    ps = pressure * scale
    return (rho * ur, mx * ur + ps * cos, my * ur + ps * sin, mz * ur, enthalpy * ur)


def axial_of(q, state, scale):
    _, mx, my, mz, _ = q
    _, _, uz, pressure, enthalpy = state
    uz = uz * scale
    return (mz * scale, mx * uz, my * uz, mz * uz + pressure * scale, enthalpy * uz)


def run_copies(copies):
    for copy in copies:
        copy.start()


def wait_copies(copies):
    for copy in copies:
        copy.wait()


def section_kernel(plan, factor, *refs):
    fields, rows, radii = plan["dims"]
    lengths, mixed, final = plan["lengths"], plan["mixed"], plan["final"]
    total = sum(lengths)
    counts = plan["counts"]
    refs = list(refs)
    flags_ref, table_ref, radius_ref, whi_hbm, wlo_hbm = refs[:5]
    del refs[:5]
    groups = []
    for count in counts:
        groups.append(refs[:count])
        del refs[:count]
    q_in, tip_in, base_in, left_in, right_in = groups
    outs = refs[: plan["outs"]]
    del refs[: plan["outs"]]
    q_s, base_s, whi_s, wlo_s, axial_s, ang_s, hi_s, lo_s, res_s, sems = refs
    lane_halves = radii // 128

    used = [0]

    def copy(src, dst):
        used[0] += 1
        return pltpu.make_async_copy(src, dst, sems.at[used[0] - 1])

    seg = flags_ref[SEG]

    def table(k, s):
        row = plan["table"] + (2 * k + s) * rows
        return jnp.concatenate([table_ref[row : row + rows]] * lane_halves, axis=1)

    def edge_table(k, side):
        row = plan["table"] + 8 * rows + (2 * k + side) * 8
        return jnp.concatenate([table_ref[row : row + 4]] * lane_halves, axis=1)

    loads, q_wait, base_wait = [], {}, {}

    kept = pl.ds(pl.multiple_of(flags_ref[HALF] * rows, rows), rows)

    def load(source, target, start, plane, at, size):
        if len(source) == 1:
            return [copy(source[0].at[:, :, start : start + size], target.at[:, :, at : at + size])]
        return [
            copy(source[0].at[:, plane : plane + size, kept], target.at[seg, :, at : at + size]),
            copy(source[1].at[:, start : start + size], target.at[1 - seg, :, at : at + size]),
        ]

    def sources(kind, held):
        held, out = list(held), []
        for width in plan["widths"][kind]:
            out.append(held[:width])
            del held[:width]
        return out

    q_from, base_from = sources("q", q_in), sources("base", base_in)
    for array, start, plane, at, size in plan["q"]:
        q_wait[at] = load(q_from[array], q_s, start, plane, at, size)
        loads += [(at, one) for one in q_wait[at]]
    if mixed:
        for array, start, plane, at, size in plan["base"]:
            base_wait[at] = load(base_from[array], base_s, start, plane, at, size)
            loads += [(at + 4, one) for one in base_wait[at]]
    weight_copies = [copy(whi_hbm, whi_s), copy(wlo_hbm, wlo_s)]
    loads += [(9, one) for one in weight_copies]
    run_copies([one for _, one in sorted(loads, key=lambda item: item[0])])

    axial_scale = (factor / 12.0) * radius_ref[...]
    radial_scale = -factor * radius_ref[...]

    def put(u, f, column, value):
        lanes = slice(column, column + value.shape[-1])
        hi = value.astype(jnp.bfloat16)
        hi_s[u, f, :, lanes] = hi
        lo_s[u, f, :, lanes] = (value - hi.astype(jnp.float32)).astype(jnp.bfloat16)

    def flux(at, u, flag):
        inner = u is not None
        tip = plan["tip"].get(at)
        if at in q_wait:
            wait_copies(q_wait[at])
        if inner:
            slot = u % 3
            edge = []
            for side, (array, start) in ((0, plan["left"][u]), (1, plan["right"][u])):
                ref = (left_in, right_in)[side][array]
                q = tuple(ref[f, start] for f in range(fields))
                edge.append(angular_of(q, speeds(q), edge_table(0, side), edge_table(1, side)))
        for s in range(2):
            if tip is None:
                q = tuple(q_s[s, f, at] for f in range(fields))
            else:
                swap_tip, other_tip = (tip_in[0], tip_in[1]) if tip[0] == "high" else (tip_in[1], tip_in[0])
                q = tuple(
                    jnp.where(flags_ref[ODD] > 0, other_tip[s, f, tip[1]], swap_tip[s, f, tip[1]])
                    for f in range(fields)
                )
            state = speeds(q)
            axial = axial_of(q, state, axial_scale)
            for f in range(fields):
                value = axial[f]
                if flag is not None:
                    value = jnp.where(flags_ref[flag] > 0, value, 0.0)
                axial_s[s, f, at] = value
            if not inner:
                continue
            radial = radial_of(q, state, table(0, s), table(1, s), radial_scale)
            for f in range(fields):
                put(u, f, 2 * radii + s * radii, radial[f])
            angular = angular_of(q, state, table(2, s), table(3, s))
            for f in range(fields):
                for l in range(lane_halves):
                    lanes = slice(l * 128, l * 128 + 128)
                    ang_s[slot, s, f, l, 8 : 8 + rows] = angular[f][:, lanes]
                    ang_s[slot, s, f, l, 6:8] = edge[0][f][2 * s : 2 * s + 2, lanes]
                    ang_s[slot, s, f, l, 8 + rows : 10 + rows] = edge[1][f][2 * s : 2 * s + 2, lanes]

    def finish(at, u):
        slot = u % 3
        if u in base_wait:
            wait_copies(base_wait[u])
        for s in range(2):
            for f in range(fields):
                for l in range(lane_halves):
                    lanes = slice(l * 128, l * 128 + 128)

                    def ang(k):
                        return ang_s[slot, s, f, l, 8 + k : 8 + k + rows]

                    def axi(k):
                        return axial_s[s, f, at + k, :, lanes]

                    near = (ang(1) - ang(-1)) + (axi(1) - axi(-1))
                    far = (ang(2) - ang(-2)) + (axi(2) - axi(-2))
                    own = q_s[s, f, at, :, lanes]
                    if mixed:
                        own = 0.5 * base_s[s, f, u, :, lanes] + 0.5 * own
                    put(u, f, s * radii + l * 128, (own - 8.0 * near) + far)

    left_swap, right_swap = flags_ref[SWAP_LEFT], flags_ref[SWAP_RIGHT]
    out_copies = []

    def multiply(first, count):
        hi = hi_s[first : first + count].reshape(count * fields * rows, 4 * radii)
        lo = lo_s[first : first + count].reshape(count * fields * rows, 4 * radii)
        dot = functools.partial(jnp.dot, preferred_element_type=jnp.float32)
        for s in range(2):
            columns = slice(s * radii, s * radii + radii)
            whi = whi_s[:, columns]
            res = dot(hi, whi) + dot(lo, whi) + dot(hi, wlo_s[:, columns])
            where = jnp.bitwise_xor(seg, s) if final else s
            for i in range(count):
                for f in range(fields):
                    start = (i * fields + f) * rows
                    res_s[where, f, first + i] = res[start : start + rows]
        if final:
            pieces = [(res_s.at[0], outs[0]), (res_s.at[1], outs[1])]
            for source, target in pieces:
                out_copies.append(
                    copy(source.at[:, first : first + count], target.at[:, first : first + count])
                )
        else:
            out_copies.append(
                copy(res_s.at[:, :, first : first + count], outs[0].at[:, :, first : first + count])
            )
            for i in range(first, first + count):
                for f in range(fields):
                    for ref, flag, start in ((outs[1], left_swap, 0), (outs[2], right_swap, rows - 2)):
                        one = res_s[0, f, i, start : start + 2]
                        two = res_s[1, f, i, start : start + 2]
                        ref[f, i, 0:2] = jnp.where(flag > 0, two, one)
                        ref[f, i, 2:4] = jnp.where(flag > 0, one, two)
        out_copies[-1].start()
        if final:
            out_copies[-2].start()

    base_at, u0, ready, done = 0, 0, 0, 0
    waited = False
    pending = []
    for r, length in enumerate(lengths):
        for t in range(length + 4):
            flag = None
            if plan["low_flag"] == r and t < 2:
                flag = 0
            if plan["high_flag"] == r and t >= length + 2:
                flag = 1
            flux(base_at + t, u0 + t - 2 if 2 <= t < length + 2 else None, flag)
            if t >= 4:
                finish(base_at + t - 2, u0 + t - 4)
                ready += 1
                if ready - done == GROUP or (ready == total and ready > done):
                    pending.append((done, ready - done))
                    done = ready
                    if len(pending) == 2:
                        if not waited:
                            wait_copies(weight_copies)
                            waited = True
                        multiply(*pending.pop(0))
        base_at += length + 4
        u0 += length
    if not waited:
        wait_copies(weight_copies)
    for item in pending:
        multiply(*item)
    if plan["tips"]:
        last = jnp.where(flags_ref[ODD] > 0, 0, total - 2)
        for target, start in ((outs[3], last), (outs[4], total - 2 - last)):
            tip = copy(res_s.at[:, :, pl.ds(start, 2)], target)
            tip.start()
            out_copies.append(tip)
    wait_copies(out_copies)


def section_task(consts, factor, ranges, q_map, base_map, left_map, right_map, flags, planes, dims, final, tips):
    fields, rows, radii = dims
    arrays = {kind: [] for kind in ("q", "tip", "base", "left", "right")}

    def index_of(kind, array):
        held = arrays[kind]
        if not any(a is array for a in held):
            held.append(array)
        return next(i for i, a in enumerate(held) if a is array)

    def flat(kind):
        return [one for a in arrays[kind] for one in (a if isinstance(a, tuple) else (a,))]

    def pieces(kind, table, wanted):
        spans = []
        for at, p in enumerate(wanted):
            array, start = table[p]
            index = index_of(kind, array)
            last = spans[-1] if spans else None
            if last and last[4] < GROUP and last[:4] == [index, start - last[4], p - last[4], at - last[4]]:
                last[4] += 1
            else:
                spans.append([index, start, p, at, 1])
        return spans

    table_row = consts[1]
    wide = [p for a, b in ranges for p in range(a - 2, b + 2)]
    tight = [p for a, b in ranges for p in range(a, b)]
    mixed = base_map is not None
    tips_at = {at: p for at, p in enumerate(wide) if p < 0 or p >= planes}
    kept = [(at, p) for at, p in enumerate(wide) if at not in tips_at]
    q_spans = pieces("q", q_map, [p for _, p in kept])
    q_spans = [[i, start, p, kept[at][0], size] for i, start, p, at, size in q_spans]
    plan = dict(
        dims=dims, lengths=[b - a for a, b in ranges], mixed=mixed, final=final, tips=tips,
        low_flag=next((i for i, r in enumerate(ranges) if r[0] == 0), None),
        high_flag=next((i for i, r in enumerate(ranges) if r[1] == planes), None),
        q=q_spans, tip={at: ("low" if p < 0 else "high", p + 2 if p < 0 else p - planes) for at, p in tips_at.items()},
        table=table_row,
        base=pieces("base", base_map, tight) if mixed else [],
        left=[(index_of("left", left_map[p][0]), left_map[p][1]) for p in tight],
        right=[(index_of("right", right_map[p][0]), right_map[p][1]) for p in tight],
    )
    kinds = ("q", "tip", "base", "left", "right")
    if tips_at:
        arrays["tip"] = list(q_map["tips"])
    plan["counts"] = [len(flat(k)) for k in kinds]
    plan["widths"] = {k: [len(a) if isinstance(a, tuple) else 1 for a in arrays[k]] for k in ("q", "base")}
    total = sum(plan["lengths"])
    spread = total + 4 * len(ranges)
    real = jax.ShapeDtypeStruct
    f32 = jnp.float32
    if final:
        out_shape = [real((fields, total, rows, radii), f32)] * 2
        out_specs = [anywhere] * 2
    else:
        out_shape = [real((2, fields, total, rows, radii), f32)] + [real((fields, total, 4, radii), f32)] * 2
        out_specs = [anywhere, vector, vector]
        if tips:
            out_shape += [real((2, fields, 2, rows, radii), f32)] * 2
            out_specs += [anywhere] * 2
    plan["outs"] = len(out_shape)
    copies = 2 * len(plan["q"]) + 2 * len(plan["base"]) + 2 + 2 * (total // GROUP + 2) + 2
    table, table_row, radius, whi, wlo = consts
    operands = [flags, table, radius, whi, wlo]
    operands += [a for k in kinds for a in flat(k)]
    places = [scalars, vector, vector, anywhere, anywhere]
    places += [vector if k in ("tip", "left", "right") else anywhere for k in kinds for _ in flat(k)]
    lines = fields * total * rows
    return pl.pallas_call(
        functools.partial(section_kernel, plan, factor),
        out_shape=out_shape,
        in_specs=places,
        out_specs=out_specs,
        scratch_shapes=[
            pltpu.VMEM((2, fields, spread, rows, radii), f32),
            pltpu.VMEM((2, fields, total, rows, radii) if mixed else (8, 128), f32),
            pltpu.VMEM(whi.shape, jnp.bfloat16),
            pltpu.VMEM(wlo.shape, jnp.bfloat16),
            pltpu.VMEM((2, fields, spread, rows, radii), f32),
            pltpu.VMEM((3, 2, fields, radii // 128, rows + 16, 128), f32),
            pltpu.VMEM((total, fields, rows, 4 * radii), jnp.bfloat16),
            pltpu.VMEM((total, fields, rows, 4 * radii), jnp.bfloat16),
            pltpu.VMEM((2, fields, total, rows, radii), f32),
            pltpu.SemaphoreType.DMA((copies,)),
        ],
        compiler_params=pltpu.CompilerParams(vmem_limit_bytes=SECTION_VMEM),
        cost_estimate=pl.CostEstimate(
            flops=2 * lines * 4 * radii * 2 * radii * 6, bytes_accessed=8 * lines * radii * 4,
            transcendentals=0,
        ),
    )(*operands)


def parts_of(spans):
    parts, at = [], 0
    for start, count in spans:
        for i in range(0, count, GROUP):
            size = min(GROUP, count - i)
            parts.append((start + i, at + i, size))
        at += count
    return parts


def edges_kernel(spans, tips, flags_ref, own_ref, far_ref, *refs):
    outs, (q_s, sems) = refs[:-2], refs[-2:]
    _, fields, planes, rows, _ = q_s.shape
    seg = flags_ref[SEG]
    parts = parts_of(spans)
    kept = pl.ds(pl.multiple_of(flags_ref[HALF] * rows, rows), rows)
    loads = []
    for i, (start, at, size) in enumerate(parts):
        span = slice(at, at + size)
        loads.append(
            [
                pltpu.make_async_copy(
                    own_ref.at[:, start : start + size, kept], q_s.at[seg, :, span], sems.at[2 * i]
                ),
                pltpu.make_async_copy(far_ref.at[:, span], q_s.at[1 - seg, :, span], sems.at[2 * i + 1]),
            ]
        )
        run_copies(loads[-1])

    def edges(p, carry):
        for f in range(fields):
            for ref, flag, start in (
                (outs[0], flags_ref[SWAP_LEFT], 0), (outs[1], flags_ref[SWAP_RIGHT], rows - 2)
            ):
                one = q_s[0, f, p, start : start + 2]
                two = q_s[1, f, p, start : start + 2]
                ref[f, p, 0:2] = jnp.where(flag > 0, two, one)
                ref[f, p, 2:4] = jnp.where(flag > 0, one, two)
        return carry

    for i, (_, at, size) in enumerate(parts):
        wait_copies(loads[i])
        lax.fori_loop(at, at + size, edges, 0)
    if tips:
        last = jnp.where(flags_ref[ODD] > 0, 0, planes - 2)
        copies = [
            pltpu.make_async_copy(
                q_s.at[:, :, pl.ds(start, 2)], outs[2 + i], sems.at[2 * len(parts) + i]
            )
            for i, start in enumerate((last, planes - 2 - last))
        ]
        run_copies(copies)
        wait_copies(copies)


def edges_task(spans, tips, flags, own, far, dims):
    fields, rows, radii = dims
    planes = far.shape[1]
    f32 = jnp.float32
    out_shape = [jax.ShapeDtypeStruct((fields, planes, 4, radii), f32)] * 2
    out_specs = [vector, vector]
    if tips:
        out_shape += [jax.ShapeDtypeStruct((2, fields, 2, rows, radii), f32)] * 2
        out_specs += [anywhere] * 2
    return pl.pallas_call(
        functools.partial(edges_kernel, spans, tips),
        out_shape=out_shape,
        in_specs=[scalars] + [anywhere] * 2,
        out_specs=out_specs,
        scratch_shapes=[
            pltpu.VMEM((2, fields, planes, rows, radii), f32),
            pltpu.SemaphoreType.DMA((2 * len(parts_of(spans)) + 2,)),
        ],
        compiler_params=pltpu.CompilerParams(vmem_limit_bytes=COPY_VMEM),
        cost_estimate=pl.CostEstimate(
            flops=0, bytes_accessed=8 * fields * planes * rows * radii, transcendentals=0
        ),
    )(flags, own, far)


def place_kernel(spans, chained, flags_ref, one_ref, two_ref, *refs):
    if chained:
        refs = refs[1:]
    out_ref, buf, sems = refs
    rows = buf.shape[2] // 2
    half = flags_ref[HALF]
    parts = parts_of(spans)
    loads = []
    for i, (_, at, size) in enumerate(parts):
        span = slice(at, at + size)
        loads.append(
            [
                pltpu.make_async_copy(
                    ref.at[:, span],
                    buf.at[:, span, pl.ds(pl.multiple_of(row * rows, rows), rows)], sems.at[2 * i + e],
                )
                for e, (ref, row) in enumerate(((one_ref, half), (two_ref, 1 - half)))
            ]
        )
        run_copies(loads[-1])
    copies = []
    for i, (first, at, size) in enumerate(parts):
        wait_copies(loads[i])
        one = pltpu.make_async_copy(
            buf.at[:, at : at + size], out_ref.at[:, first : first + size], sems.at[2 * len(parts) + i]
        )
        one.start()
        copies.append(one)
    wait_copies(copies)


def place_task(spans, flags, one, two, whole, shape):
    fields, _, ang_dev, radii = shape
    count = sum(n for _, n in spans)
    operands = [flags, one, two] + ([] if whole is None else [whole])
    return pl.pallas_call(
        functools.partial(place_kernel, spans, whole is not None),
        out_shape=jax.ShapeDtypeStruct(shape, jnp.float32),
        in_specs=[scalars] + [anywhere] * (len(operands) - 1),
        out_specs=anywhere,
        scratch_shapes=[
            pltpu.VMEM((fields, count, ang_dev, radii), jnp.float32),
            pltpu.SemaphoreType.DMA((3 * len(parts_of(spans)),)),
        ],
        compiler_params=pltpu.CompilerParams(vmem_limit_bytes=COPY_VMEM),
        input_output_aliases={} if whole is None else {3: 0},
        cost_estimate=pl.CostEstimate(
            flops=0, bytes_accessed=8 * fields * count * ang_dev * radii, transcendentals=0
        ),
    )(*operands)


def per_device(conserved, deriv_matrix, filter_matrix):
    n = lax.axis_size("ang")
    count = lax.axis_size("ax")
    fields, planes, ang_dev, radii = conserved.shape
    rows = ang_dev // 2
    dims = (fields, rows, radii)
    half = n // 2
    total = ang_dev * n
    twist = total / (2.0 * math.pi * radii)
    pos = lax.axis_index("ang")
    layer = lax.axis_index("ax")
    h, pair = pos // half, pos % half
    kept = h ^ (pair & 1)
    ring = 2 * pair + kept
    across = [(i, (i + half) % n) for i in range(n)]
    order = [((r % 2) ^ (r // 2 & 1)) * half + r // 2 for r in range(n)]
    to_left = [(order[r], order[(r - 1) % n]) for r in range(n)]
    to_right = [(order[r], order[(r + 1) % n]) for r in range(n)]

    def layer_swap(first):
        table = {i: i for i in range(count)}
        for i in range(first, count - 1, 2):
            table[i], table[i + 1] = i + 1, i
        return sorted(table.items())

    flags = jnp.stack(
        [layer > 0, layer < count - 1, ring == 0, ring == n - 1, h == 1, layer % 2 == 1, kept == 1]
    ).astype(jnp.int32)

    def angles(offsets):
        index = (ring * rows + offsets) % total
        return index.astype(jnp.float32) * (2.0 * math.pi / total)

    seg = jnp.arange(2, dtype=jnp.int32)[:, None] * (total // 2)
    centre = angles(seg + jnp.arange(rows, dtype=jnp.int32))
    left_rows = angles((seg + jnp.arange(-2, 0, dtype=jnp.int32)).reshape(4))
    right_rows = angles((seg + jnp.arange(rows, rows + 2, dtype=jnp.int32)).reshape(4))
    edges = jnp.stack([left_rows, right_rows])

    def trig_rows(weight):
        scale = weight * courant * twist / 12.0
        inner = jnp.stack([jnp.cos(centre), jnp.sin(centre)])
        outer_rows = jnp.pad(scale * jnp.stack([jnp.cos(edges), jnp.sin(edges)]), ((0, 0), (0, 0), (0, 4)))
        return jnp.concatenate([inner.reshape(-1), (scale * inner).reshape(-1), outer_rows.reshape(-1)])

    trig_values = jnp.concatenate([trig_rows(1.0), trig_rows(0.5)])
    table = jnp.broadcast_to(trig_values[:, None], (trig_values.shape[0], 128))
    radius = ((jnp.arange(radii, dtype=jnp.int32).astype(jnp.float32) + 0.5) / radii)[None]
    outer = OUTER * planes // 24
    span_outer = ((0, outer), (planes - outer, outer))
    span_inner = ((outer, planes - 2 * outer),)

    def send(spans):
        block = cut_task(spans, flags, conserved)
        return lax.ppermute(block, "ang", across)

    def trade(left_edge, right_edge):
        left = lax.ppermute(right_edge, "ang", to_right)
        return left, lax.ppermute(left_edge, "ang", to_left)

    def trade_tips(one, two):
        one = lax.ppermute(one, "ax", layer_swap(0))
        return one, lax.ppermute(two, "ax", layer_swap(1))

    def listed(array, ranges):
        at, table = 0, {}
        for a, b in ranges:
            for p in range(a, b):
                table[p] = (array, at)
                at += 1
        return table

    sent_outer = send(span_outer)
    sent_inner = send(span_inner)

    flags, whi, wlo = prepare(flags, filter_matrix, deriv_matrix, table, radius)

    ro = ((0, outer), (planes - outer, planes))
    ri = ((outer, planes - outer),)
    one_o = ((0, outer - 2), (planes - outer + 2, planes))
    one_i = ((outer - 2, planes - outer + 2),)
    two_o = ((0, outer - 4), (planes - outer + 4, planes))
    cuts = [outer - 4 + (planes - 2 * outer + 8) * i // TAILS for i in range(TAILS + 1)]

    def section(weight, ranges, maps, base_map, final=False, tips=False):
        q_map, left_map, right_map = maps
        return section_task(
            (table, 0 if weight == 1.0 else trig_values.shape[0] // 2, radius, whi, wlo), weight * courant, ranges, q_map, base_map, left_map,
            right_map, flags, planes, dims, final, tips,
        )

    left_o, right_o, tip_one, tip_two = edges_task(span_outer, True, flags, conserved, sent_outer, dims)
    halo_left, halo_right = trade(left_o, right_o)
    q_map = listed((conserved, sent_outer), ro)
    q_map["tips"] = trade_tips(tip_one, tip_two)
    lefts, rights = listed(halo_left, ro), listed(halo_right, ro)
    f_o, left_f, right_f, tip_one, tip_two = section(1.0, one_o, (q_map, lefts, rights), None, tips=True)
    halo_left, halo_right = trade(left_f, right_f)
    f_map = listed(f_o, one_o)
    f_map["tips"] = trade_tips(tip_one, tip_two)
    f_lefts, f_rights = listed(halo_left, one_o), listed(halo_right, one_o)

    left_i, right_i = edges_task(span_inner, False, flags, conserved, sent_inner, dims)
    halo_left, halo_right = trade(left_i, right_i)
    q_map.update(listed((conserved, sent_inner), ri))
    lefts.update(listed(halo_left, ri))
    rights.update(listed(halo_right, ri))

    def give_back(near, far):
        return near, lax.ppermute(far, "ang", across)

    backs = []
    near, far = section(0.5, two_o, (f_map, f_lefts, f_rights), q_map, final=True)
    backs.append((two_o, give_back(near, far)))

    f_i, left_f, right_f = section(1.0, one_i, (q_map, lefts, rights), None)
    halo_left, halo_right = trade(left_f, right_f)
    f_map.update(listed(f_i, one_i))
    f_lefts.update(listed(halo_left, one_i))
    f_rights.update(listed(halo_right, one_i))
    for i in range(TAILS):
        ranges = ((cuts[i], cuts[i + 1]),)
        near, far = section(0.5, ranges, (f_map, f_lefts, f_rights), q_map, final=True)
        backs.append((ranges, give_back(near, far)))

    out = None
    for ranges, arrived in backs:
        spans = tuple((a, b - a) for a, b in ranges)
        out = place_task(spans, flags, *arrived, out, conserved.shape)
    return out


def solution(mesh):
    placed = (P(None, "ax", "ang", None), P(), P())

    return jax.shard_map(
        per_device,
        mesh=mesh,
        in_specs=placed,
        out_specs=P(None, "ax", "ang", None),
        check_vma=False,
    )
```

```python
import functools
import math

import jax
import jax.numpy as jnp
from jax import lax
from jax.experimental import pallas as pl
from jax.experimental.pallas import tpu as pltpu
from jax.sharding import PartitionSpec as P


gamma_ratio = 1.4
courant = 0.15
anywhere = pl.BlockSpec(memory_space=pl.ANY)
scalars = pl.BlockSpec(memory_space=pltpu.SMEM)
vector = pl.BlockSpec(memory_space=pltpu.VMEM)
GROUP = 4
TAILS = 3
OUTER = 7
SECTION_VMEM = 28 << 20
COPY_VMEM = 8 << 20


def prepare_kernel(flags_ref, filter_ref, deriv_ref, table_ref, radius_ref, flags_out, hi_ref, lo_ref):
    for i in range(flags_ref.shape[0]):
        flags_out[i] = flags_ref[i]
    size = filter_ref.shape[0]
    half = size // 2
    dot = functools.partial(jnp.dot, preferred_element_type=jnp.float32)

    def fold(flip):
        row = lax.broadcasted_iota(jnp.int32, (size, size), flip)
        column = lax.broadcasted_iota(jnp.int32, (size, size), 1 - flip)
        return (column == jnp.where(row < half, row + half, size - 1 - row)).astype(jnp.bfloat16)

    into, back_out = fold(0), fold(1)

    def split(value):
        hi = value.astype(jnp.bfloat16)
        return hi, (value - hi.astype(jnp.float32)).astype(jnp.bfloat16)

    def folded(matrix):
        turned = lax.dot_general(
            into, matrix, (((1,), (1,)), ((), ())), preferred_element_type=jnp.float32
        ).astype(jnp.bfloat16)
        return dot(turned, back_out)

    filter_hi, filter_lo = (folded(part) for part in split(filter_ref[...]))
    deriv_hi, deriv_lo = (folded(part).astype(jnp.bfloat16) for part in split(deriv_ref[...]))
    hi_ref[:size] = filter_hi.astype(jnp.bfloat16)
    lo_ref[:size] = filter_lo.astype(jnp.bfloat16)
    row = lax.broadcasted_iota(jnp.int32, (size, size), 0)
    sign = jnp.where(row < half, 1.0, -1.0)
    signed_hi = (sign * filter_hi).astype(jnp.bfloat16)
    signed_lo = (sign * filter_lo).astype(jnp.bfloat16)
    both = dot(deriv_hi, signed_hi) + dot(deriv_lo, signed_hi) + dot(deriv_hi, signed_lo)
    hi, lo = split(both)
    hi_ref[size:] = hi
    lo_ref[size:] = lo


def prepare(flags, filter_matrix, deriv_matrix, table, radius):
    size = filter_matrix.shape[0]
    half = jax.ShapeDtypeStruct((2 * size, size), jnp.bfloat16)
    return pl.pallas_call(
        prepare_kernel,
        out_shape=(jax.ShapeDtypeStruct(flags.shape, flags.dtype), half, half),
        in_specs=[scalars, vector, vector, anywhere, anywhere],
        out_specs=(scalars, vector, vector),
        compiler_params=pltpu.CompilerParams(vmem_limit_bytes=3 * COPY_VMEM),
        name="prepare",
    )(flags, filter_matrix, deriv_matrix, table, radius)


def cut_kernel(spans, flags_ref, own_ref, out_ref, sems):
    rows = out_ref.shape[2]
    half = 1 - flags_ref[HALF]
    copies = []
    for i, (start, at, size) in enumerate(parts_of(spans)):
        copies.append(
            pltpu.make_async_copy(
                own_ref.at[:, start : start + size, pl.ds(pl.multiple_of(half * rows, rows), rows)],
                out_ref.at[:, at : at + size], sems.at[i],
            )
        )
    run_copies(copies)
    wait_copies(copies)


def cut_task(spans, flags, own):
    fields, _, both, radii = own.shape
    planes = sum(count for _, count in spans)
    return pl.pallas_call(
        functools.partial(cut_kernel, spans),
        out_shape=jax.ShapeDtypeStruct((fields, planes, both // 2, radii), own.dtype),
        in_specs=[scalars, pl.BlockSpec(memory_space=pltpu.HBM)], out_specs=vector,
        scratch_shapes=[pltpu.SemaphoreType.DMA((len(parts_of(spans)),))],
        compiler_params=pltpu.CompilerParams(vmem_limit_bytes=COPY_VMEM),
        cost_estimate=pl.CostEstimate(
            flops=0, bytes_accessed=4 * fields * planes * both * radii, transcendentals=0
        ),
    )(flags, own)


_, _, SWAP_LEFT, SWAP_RIGHT, SEG, ODD, HALF = range(7)


def speeds(q):
    rho, mx, my, mz, en = q
    inv = 1.0 / rho
    ux, uy, uz = mx * inv, my * inv, mz * inv
    pressure = (gamma_ratio - 1.0) * (en - 0.5 * (mx * ux + my * uy + mz * uz))
    return ux, uy, uz, pressure, en + pressure


def angular_of(q, state, cos, sin):
    rho, mx, my, mz, _ = q
    ux, uy, _, pressure, enthalpy = state
    us = uy * cos - ux * sin
    return (rho * us, mx * us - pressure * sin, my * us + pressure * cos, mz * us, enthalpy * us)


def radial_of(q, state, cos, sin, scale):
    rho, mx, my, mz, _ = q
    ux, uy, _, pressure, enthalpy = state
    ur = (ux * cos + uy * sin) * scale
    ps = pressure * scale
    return (rho * ur, mx * ur + ps * cos, my * ur + ps * sin, mz * ur, enthalpy * ur)


def axial_of(q, state, scale):
    _, mx, my, mz, _ = q
    _, _, uz, pressure, enthalpy = state
    uz = uz * scale
    return (mz * scale, mx * uz, my * uz, mz * uz + pressure * scale, enthalpy * uz)


def run_copies(copies):
    for copy in copies:
        copy.start()


def wait_copies(copies):
    for copy in copies:
        copy.wait()


def section_kernel(plan, factor, *refs):
    fields, rows, radii = plan["dims"]
    lengths, mixed, final = plan["lengths"], plan["mixed"], plan["final"]
    total = sum(lengths)
    counts = plan["counts"]
    refs = list(refs)
    flags_ref, table_ref, radius_ref, whi_hbm, wlo_hbm = refs[:5]
    del refs[:5]
    groups = []
    for count in counts:
        groups.append(refs[:count])
        del refs[:count]
    q_in, tip_in, base_in, left_in, right_in = groups
    outs = refs[: plan["outs"]]
    del refs[: plan["outs"]]
    q_s, base_s, whi_s, wlo_s, axial_s, ang_s, hi_s, lo_s, res_s, sems = refs
    lane_halves = radii // 128

    used = [0]

    def copy(src, dst):
        used[0] += 1
        return pltpu.make_async_copy(src, dst, sems.at[used[0] - 1])

    seg = flags_ref[SEG]

    def table(k, s):
        row = plan["table"] + (2 * k + s) * rows
        return jnp.concatenate([table_ref[row : row + rows]] * lane_halves, axis=1)

    def edge_table(k, side):
        row = plan["table"] + 8 * rows + (2 * k + side) * 8
        return jnp.concatenate([table_ref[row : row + 4]] * lane_halves, axis=1)

    loads, q_wait, base_wait = [], {}, {}

    kept = pl.ds(pl.multiple_of(flags_ref[HALF] * rows, rows), rows)

    def load(source, target, start, plane, at, size):
        if len(source) == 1:
            return [copy(source[0].at[:, :, start : start + size], target.at[:, :, at : at + size])]
        return [
            copy(source[0].at[:, plane : plane + size, kept], target.at[seg, :, at : at + size]),
            copy(source[1].at[:, start : start + size], target.at[1 - seg, :, at : at + size]),
        ]

    def sources(kind, held):
        held, out = list(held), []
        for width in plan["widths"][kind]:
            out.append(held[:width])
            del held[:width]
        return out

    q_from, base_from = sources("q", q_in), sources("base", base_in)
    for array, start, plane, at, size in plan["q"]:
        q_wait[at] = load(q_from[array], q_s, start, plane, at, size)
        loads += [(at, one) for one in q_wait[at]]
    if mixed:
        for array, start, plane, at, size in plan["base"]:
            base_wait[at] = load(base_from[array], base_s, start, plane, at, size)
            loads += [(at + 4, one) for one in base_wait[at]]
    weight_copies = [copy(whi_hbm, whi_s), copy(wlo_hbm, wlo_s)]
    loads += [(9, one) for one in weight_copies]
    run_copies([one for _, one in sorted(loads, key=lambda item: item[0])])

    axial_scale = (factor / 12.0) * radius_ref[...]
    radial_scale = -factor * radius_ref[...]

    def put(u, f, column, value):
        lanes = slice(column, column + value.shape[-1])
        hi = value.astype(jnp.bfloat16)
        hi_s[u, f, :, lanes] = hi
        lo_s[u, f, :, lanes] = (value - hi.astype(jnp.float32)).astype(jnp.bfloat16)

    def tip_value(s, f, tip):
        high = tip[0] == "high"

        def picked(pair, *at):
            swapped, other = pair if high else pair[::-1]
            return jnp.where(flags_ref[ODD] > 0, other[*at], swapped[*at])

        if len(tip_in) == 2:
            return picked(tip_in, s, f, tip[1])
        near, far = picked(tip_in[:2], f, tip[1]), picked(tip_in[2:], f, tip[1])
        return jnp.where(seg == s, near, far)

    def flux(at, u, flag):
        inner = u is not None
        tip = plan["tip"].get(at)
        if at in q_wait:
            wait_copies(q_wait[at])
        if inner:
            slot = u % 3
            (array, start), (other, other_start) = plan["left"][u], plan["right"][u]
            sides = [
                tuple(left_in[array][f, start] for f in range(fields)),
                tuple(right_in[other][f, other_start] for f in range(fields)),
            ]
            if plan["by_kind"]:
                inner_edge, outer_edge = sides
                upper = flags_ref[HALF] > 0
                sides = [
                    tuple(jnp.where(upper, i, o) for i, o in zip(inner_edge, outer_edge)),
                    tuple(jnp.where(upper, o, i) for i, o in zip(inner_edge, outer_edge)),
                ]
            edge = [
                angular_of(q, speeds(q), edge_table(0, side), edge_table(1, side))
                for side, q in enumerate(sides)
            ]
        for s in range(2):
            if tip is None:
                q = tuple(q_s[s, f, at] for f in range(fields))
            else:
                q = tuple(tip_value(s, f, tip) for f in range(fields))
            state = speeds(q)
            axial = axial_of(q, state, axial_scale)
            for f in range(fields):
                value = axial[f]
                if flag is not None:
                    value = jnp.where(flags_ref[flag] > 0, value, 0.0)
                axial_s[s, f, at] = value
            if not inner:
                continue
            radial = radial_of(q, state, table(0, s), table(1, s), radial_scale)
            for f in range(fields):
                put(u, f, 2 * radii + s * radii, radial[f])
            angular = angular_of(q, state, table(2, s), table(3, s))
            for f in range(fields):
                for l in range(lane_halves):
                    lanes = slice(l * 128, l * 128 + 128)
                    ang_s[slot, s, f, l, 8 : 8 + rows] = angular[f][:, lanes]
                    ang_s[slot, s, f, l, 6:8] = edge[0][f][2 * s : 2 * s + 2, lanes]
                    ang_s[slot, s, f, l, 8 + rows : 10 + rows] = edge[1][f][2 * s : 2 * s + 2, lanes]

    def finish(at, u):
        slot = u % 3
        if u in base_wait:
            wait_copies(base_wait[u])
        for s in range(2):
            for f in range(fields):
                for l in range(lane_halves):
                    lanes = slice(l * 128, l * 128 + 128)

                    def ang(k):
                        return ang_s[slot, s, f, l, 8 + k : 8 + k + rows]

                    def axi(k):
                        return axial_s[s, f, at + k, :, lanes]

                    near = (ang(1) - ang(-1)) + (axi(1) - axi(-1))
                    far = (ang(2) - ang(-2)) + (axi(2) - axi(-2))
                    own = q_s[s, f, at, :, lanes]
                    if mixed:
                        own = 0.5 * base_s[s, f, u, :, lanes] + 0.5 * own
                    put(u, f, s * radii + l * 128, (own - 8.0 * near) + far)

    left_swap, right_swap = flags_ref[SWAP_LEFT], flags_ref[SWAP_RIGHT]
    out_copies = []

    def multiply(first, count):
        hi = hi_s[first : first + count].reshape(count * fields * rows, 4 * radii)
        lo = lo_s[first : first + count].reshape(count * fields * rows, 4 * radii)
        dot = functools.partial(jnp.dot, preferred_element_type=jnp.float32)
        for s in range(2):
            columns = slice(s * radii, s * radii + radii)
            whi = whi_s[:, columns]
            res = dot(hi, whi) + dot(lo, whi) + dot(hi, wlo_s[:, columns])
            where = jnp.bitwise_xor(seg, s) if final else s
            for i in range(count):
                for f in range(fields):
                    start = (i * fields + f) * rows
                    res_s[where, f, first + i] = res[start : start + rows]
        if final:
            pieces = [(res_s.at[0], outs[0]), (res_s.at[1], outs[1])]
            for source, target in pieces:
                out_copies.append(
                    copy(source.at[:, first : first + count], target.at[:, first : first + count])
                )
        else:
            out_copies.append(
                copy(res_s.at[:, :, first : first + count], outs[0].at[:, :, first : first + count])
            )
            for i in range(first, first + count):
                for f in range(fields):
                    for ref, flag, start in ((outs[1], left_swap, 0), (outs[2], right_swap, rows - 2)):
                        one = res_s[0, f, i, start : start + 2]
                        two = res_s[1, f, i, start : start + 2]
                        ref[f, i, 0:2] = jnp.where(flag > 0, two, one)
                        ref[f, i, 2:4] = jnp.where(flag > 0, one, two)
        out_copies[-1].start()
        if final:
            out_copies[-2].start()

    base_at, u0, ready, done = 0, 0, 0, 0
    waited = False
    pending = []
    for r, length in enumerate(lengths):
        for t in range(length + 4):
            flag = None
            if plan["low_flag"] == r and t < 2:
                flag = 0
            if plan["high_flag"] == r and t >= length + 2:
                flag = 1
            flux(base_at + t, u0 + t - 2 if 2 <= t < length + 2 else None, flag)
            if t >= 4:
                finish(base_at + t - 2, u0 + t - 4)
                ready += 1
                if ready - done == GROUP or (ready == total and ready > done):
                    pending.append((done, ready - done))
                    done = ready
                    if len(pending) == 2:
                        if not waited:
                            wait_copies(weight_copies)
                            waited = True
                        multiply(*pending.pop(0))
        base_at += length + 4
        u0 += length
    if not waited:
        wait_copies(weight_copies)
    for item in pending:
        multiply(*item)
    if plan["tips"]:
        last = jnp.where(flags_ref[ODD] > 0, 0, total - 2)
        for target, start in ((outs[3], last), (outs[4], total - 2 - last)):
            tip = copy(res_s.at[:, :, pl.ds(start, 2)], target)
            tip.start()
            out_copies.append(tip)
    wait_copies(out_copies)


def section_task(consts, factor, ranges, q_map, base_map, left_map, right_map, flags, planes, dims, final, tips):
    fields, rows, radii = dims
    arrays = {kind: [] for kind in ("q", "tip", "base", "left", "right")}

    def index_of(kind, array):
        held = arrays[kind]
        if not any(a is array for a in held):
            held.append(array)
        return next(i for i, a in enumerate(held) if a is array)

    def flat(kind):
        return [one for a in arrays[kind] for one in (a if isinstance(a, tuple) else (a,))]

    def pieces(kind, table, wanted):
        spans = []
        for at, p in enumerate(wanted):
            array, start = table[p]
            index = index_of(kind, array)
            last = spans[-1] if spans else None
            if last and last[4] < GROUP and last[:4] == [index, start - last[4], p - last[4], at - last[4]]:
                last[4] += 1
            else:
                spans.append([index, start, p, at, 1])
        return spans

    table_row = consts[1]
    wide = [p for a, b in ranges for p in range(a - 2, b + 2)]
    tight = [p for a, b in ranges for p in range(a, b)]
    mixed = base_map is not None
    tips_at = {at: p for at, p in enumerate(wide) if p < 0 or p >= planes}
    kept = [(at, p) for at, p in enumerate(wide) if at not in tips_at]
    q_spans = pieces("q", q_map, [p for _, p in kept])
    q_spans = [[i, start, p, kept[at][0], size] for i, start, p, at, size in q_spans]
    plan = dict(
        dims=dims, lengths=[b - a for a, b in ranges], mixed=mixed, final=final, tips=tips,
        low_flag=next((i for i, r in enumerate(ranges) if r[0] == 0), None),
        high_flag=next((i for i, r in enumerate(ranges) if r[1] == planes), None),
        q=q_spans, tip={at: ("low" if p < 0 else "high", p + 2 if p < 0 else p - planes) for at, p in tips_at.items()},
        table=table_row, by_kind=not mixed,
        base=pieces("base", base_map, tight) if mixed else [],
        left=[(index_of("left", left_map[p][0]), left_map[p][1]) for p in tight],
        right=[(index_of("right", right_map[p][0]), right_map[p][1]) for p in tight],
    )
    kinds = ("q", "tip", "base", "left", "right")
    if tips_at:
        arrays["tip"] = list(q_map["tips"])
    plan["counts"] = [len(flat(k)) for k in kinds]
    plan["widths"] = {k: [len(a) if isinstance(a, tuple) else 1 for a in arrays[k]] for k in ("q", "base")}
    total = sum(plan["lengths"])
    spread = total + 4 * len(ranges)
    real = jax.ShapeDtypeStruct
    f32 = jnp.float32
    if final:
        out_shape = [real((fields, total, rows, radii), f32)] * 2
        out_specs = [anywhere] * 2
    else:
        out_shape = [real((2, fields, total, rows, radii), f32)] + [real((fields, total, 4, radii), f32)] * 2
        out_specs = [anywhere, vector, vector]
        if tips:
            out_shape += [real((2, fields, 2, rows, radii), f32)] * 2
            out_specs += [anywhere] * 2
    plan["outs"] = len(out_shape)
    copies = 2 * len(plan["q"]) + 2 * len(plan["base"]) + 2 + 2 * (total // GROUP + 2) + 2
    table, table_row, radius, whi, wlo = consts
    operands = [flags, table, radius, whi, wlo]
    operands += [a for k in kinds for a in flat(k)]
    places = [scalars, vector, vector, anywhere, anywhere]
    places += [vector if k in ("tip", "left", "right") else anywhere for k in kinds for _ in flat(k)]
    lines = fields * total * rows
    return pl.pallas_call(
        functools.partial(section_kernel, plan, factor),
        out_shape=out_shape,
        in_specs=places,
        out_specs=out_specs,
        scratch_shapes=[
            pltpu.VMEM((2, fields, spread, rows, radii), f32),
            pltpu.VMEM((2, fields, total, rows, radii) if mixed else (8, 128), f32),
            pltpu.VMEM(whi.shape, jnp.bfloat16),
            pltpu.VMEM(wlo.shape, jnp.bfloat16),
            pltpu.VMEM((2, fields, spread, rows, radii), f32),
            pltpu.VMEM((3, 2, fields, radii // 128, rows + 16, 128), f32),
            pltpu.VMEM((total, fields, rows, 4 * radii), jnp.bfloat16),
            pltpu.VMEM((total, fields, rows, 4 * radii), jnp.bfloat16),
            pltpu.VMEM((2, fields, total, rows, radii), f32),
            pltpu.SemaphoreType.DMA((copies,)),
        ],
        compiler_params=pltpu.CompilerParams(vmem_limit_bytes=SECTION_VMEM),
        cost_estimate=pl.CostEstimate(
            flops=2 * lines * 4 * radii * 2 * radii * 6, bytes_accessed=8 * lines * radii * 4,
            transcendentals=0,
        ),
    )(*operands)


def parts_of(spans):
    parts, at = [], 0
    for start, count in spans:
        for i in range(0, count, GROUP):
            size = min(GROUP, count - i)
            parts.append((start + i, at + i, size))
        at += count
    return parts


def edges_kernel(spans, tips, flags_ref, own_ref, far_ref, *refs):
    outs, (q_s, sems) = refs[:-2], refs[-2:]
    _, fields, planes, rows, _ = q_s.shape
    seg = flags_ref[SEG]
    parts = parts_of(spans)
    kept = pl.ds(pl.multiple_of(flags_ref[HALF] * rows, rows), rows)
    loads = []
    for i, (start, at, size) in enumerate(parts):
        span = slice(at, at + size)
        loads.append(
            [
                pltpu.make_async_copy(
                    own_ref.at[:, start : start + size, kept], q_s.at[seg, :, span], sems.at[2 * i]
                ),
                pltpu.make_async_copy(far_ref.at[:, span], q_s.at[1 - seg, :, span], sems.at[2 * i + 1]),
            ]
        )
        run_copies(loads[-1])

    last_half, swapped = flags_ref[HALF], flags_ref[SWAP_LEFT] + flags_ref[SWAP_RIGHT]

    def edges(p, carry):
        for f in range(fields):
            one, two = (
                jnp.where(last_half > 0, q_s[s, f, p, rows - 2 : rows], q_s[s, f, p, 0:2]) for s in range(2)
            )
            outs[0][f, p, 0:2] = jnp.where(swapped > 0, two, one)
            outs[0][f, p, 2:4] = jnp.where(swapped > 0, one, two)
        return carry

    for i, (_, at, size) in enumerate(parts):
        wait_copies(loads[i])
        lax.fori_loop(at, at + size, edges, 0)
    if tips:
        last = jnp.where(flags_ref[ODD] > 0, 0, planes - 2)
        copies = [
            pltpu.make_async_copy(
                q_s.at[1 - seg, :, pl.ds(start, 2)], outs[1 + i], sems.at[2 * len(parts) + i]
            )
            for i, start in enumerate((last, planes - 2 - last))
        ]
        run_copies(copies)
        wait_copies(copies)


def edges_task(spans, tips, flags, own, far, dims):
    fields, rows, radii = dims
    planes = far.shape[1]
    f32 = jnp.float32
    out_shape = [jax.ShapeDtypeStruct((fields, planes, 4, radii), f32)]
    out_specs = [vector]
    if tips:
        out_shape += [jax.ShapeDtypeStruct((fields, 2, rows, radii), f32)] * 2
        out_specs += [anywhere] * 2
    return pl.pallas_call(
        functools.partial(edges_kernel, spans, tips),
        out_shape=out_shape,
        in_specs=[scalars] + [anywhere] * 2,
        out_specs=out_specs,
        scratch_shapes=[
            pltpu.VMEM((2, fields, planes, rows, radii), f32),
            pltpu.SemaphoreType.DMA((2 * len(parts_of(spans)) + 2,)),
        ],
        compiler_params=pltpu.CompilerParams(vmem_limit_bytes=COPY_VMEM),
        cost_estimate=pl.CostEstimate(
            flops=0, bytes_accessed=8 * fields * planes * rows * radii, transcendentals=0
        ),
    )(flags, own, far)


def place_kernel(spans, chained, flags_ref, one_ref, two_ref, *refs):
    if chained:
        refs = refs[1:]
    out_ref, buf, sems = refs
    rows = buf.shape[2] // 2
    half = flags_ref[HALF]
    parts = parts_of(spans)
    loads = []
    for i, (_, at, size) in enumerate(parts):
        span = slice(at, at + size)
        loads.append(
            [
                pltpu.make_async_copy(
                    ref.at[:, span],
                    buf.at[:, span, pl.ds(pl.multiple_of(row * rows, rows), rows)], sems.at[2 * i + e],
                )
                for e, (ref, row) in enumerate(((one_ref, half), (two_ref, 1 - half)))
            ]
        )
        run_copies(loads[-1])
    copies = []
    for i, (first, at, size) in enumerate(parts):
        wait_copies(loads[i])
        one = pltpu.make_async_copy(
            buf.at[:, at : at + size], out_ref.at[:, first : first + size], sems.at[2 * len(parts) + i]
        )
        one.start()
        copies.append(one)
    wait_copies(copies)


def place_task(spans, flags, one, two, whole, shape):
    fields, _, ang_dev, radii = shape
    count = sum(n for _, n in spans)
    operands = [flags, one, two] + ([] if whole is None else [whole])
    return pl.pallas_call(
        functools.partial(place_kernel, spans, whole is not None),
        out_shape=jax.ShapeDtypeStruct(shape, jnp.float32),
        in_specs=[scalars] + [anywhere] * (len(operands) - 1),
        out_specs=anywhere,
        scratch_shapes=[
            pltpu.VMEM((fields, count, ang_dev, radii), jnp.float32),
            pltpu.SemaphoreType.DMA((3 * len(parts_of(spans)),)),
        ],
        compiler_params=pltpu.CompilerParams(vmem_limit_bytes=COPY_VMEM),
        input_output_aliases={} if whole is None else {3: 0},
        cost_estimate=pl.CostEstimate(
            flops=0, bytes_accessed=8 * fields * count * ang_dev * radii, transcendentals=0
        ),
    )(*operands)


def per_device(conserved, deriv_matrix, filter_matrix):
    n = lax.axis_size("ang")
    count = lax.axis_size("ax")
    fields, planes, ang_dev, radii = conserved.shape
    rows = ang_dev // 2
    dims = (fields, rows, radii)
    half = n // 2
    total = ang_dev * n
    twist = total / (2.0 * math.pi * radii)
    pos = lax.axis_index("ang")
    layer = lax.axis_index("ax")
    h, pair = pos // half, pos % half
    kept = h ^ (pair & 1)
    ring = 2 * pair + kept
    across = [(i, (i + half) % n) for i in range(n)]
    order = [((r % 2) ^ (r // 2 & 1)) * half + r // 2 for r in range(n)]
    to_left = [(order[r], order[(r - 1) % n]) for r in range(n)]
    to_right = [(order[r], order[(r + 1) % n]) for r in range(n)]
    beside = [(order[r], order[(r + 1 if r % 2 else r - 1) % n]) for r in range(n)]

    def layer_swap(first):
        table = {i: i for i in range(count)}
        for i in range(first, count - 1, 2):
            table[i], table[i + 1] = i + 1, i
        return sorted(table.items())

    flags = jnp.stack(
        [layer > 0, layer < count - 1, ring == 0, ring == n - 1, h == 1, layer % 2 == 1, kept == 1]
    ).astype(jnp.int32)

    def angles(offsets):
        index = (ring * rows + offsets) % total
        return index.astype(jnp.float32) * (2.0 * math.pi / total)

    seg = jnp.arange(2, dtype=jnp.int32)[:, None] * (total // 2)
    centre = angles(seg + jnp.arange(rows, dtype=jnp.int32))
    left_rows = angles((seg + jnp.arange(-2, 0, dtype=jnp.int32)).reshape(4))
    right_rows = angles((seg + jnp.arange(rows, rows + 2, dtype=jnp.int32)).reshape(4))
    edges = jnp.stack([left_rows, right_rows])

    def trig_rows(weight):
        scale = weight * courant * twist / 12.0
        inner = jnp.stack([jnp.cos(centre), jnp.sin(centre)])
        outer_rows = jnp.pad(scale * jnp.stack([jnp.cos(edges), jnp.sin(edges)]), ((0, 0), (0, 0), (0, 4)))
        return jnp.concatenate([inner.reshape(-1), (scale * inner).reshape(-1), outer_rows.reshape(-1)])

    trig_values = jnp.concatenate([trig_rows(1.0), trig_rows(0.5)])
    table = jnp.broadcast_to(trig_values[:, None], (trig_values.shape[0], 128))
    radius = ((jnp.arange(radii, dtype=jnp.int32).astype(jnp.float32) + 0.5) / radii)[None]
    outer = OUTER * planes // 24
    span_outer = ((0, outer), (planes - outer, outer))
    span_inner = ((outer, planes - 2 * outer),)

    def send(spans):
        block = cut_task(spans, flags, conserved)
        return lax.ppermute(block, "ang", across)

    def trade(left_edge, right_edge):
        left = lax.ppermute(right_edge, "ang", to_right)
        return left, lax.ppermute(left_edge, "ang", to_left)

    def trade_tips(one, two):
        one = lax.ppermute(one, "ax", layer_swap(0))
        return one, lax.ppermute(two, "ax", layer_swap(1))

    def listed(array, ranges):
        at, table = 0, {}
        for a, b in ranges:
            for p in range(a, b):
                table[p] = (array, at)
                at += 1
        return table

    sent_outer = send(span_outer)
    low_rows, high_rows = conserved[:, :, rows - 2 : rows], conserved[:, :, rows : rows + 2]
    far_rows = lax.ppermute(jnp.where(kept == 0, low_rows, high_rows), "ang", across)
    own_rows = jnp.where(kept == 0, high_rows, low_rows)
    inner_rows = jnp.concatenate(
        [jnp.where(h == 0, own_rows, far_rows), jnp.where(h == 0, far_rows, own_rows)], axis=2
    )

    def own_tip(start):
        block = conserved[:, start : start + 2]
        return jnp.where(kept == 0, block[:, :, :rows], block[:, :, rows:])

    own_low, own_high = own_tip(0), own_tip(planes - 2)
    odd_layer = layer % 2 == 1
    near_tips = (
        lax.ppermute(jnp.where(odd_layer, own_low, own_high), "ax", layer_swap(0)),
        lax.ppermute(jnp.where(odd_layer, own_high, own_low), "ax", layer_swap(1)),
    )
    sent_inner = send(span_inner)

    flags, whi, wlo = prepare(flags, filter_matrix, deriv_matrix, table, radius)

    ro = ((0, outer), (planes - outer, planes))
    ri = ((outer, planes - outer),)
    one_o = ((0, outer - 2), (planes - outer + 2, planes))
    one_i = ((outer - 2, planes - outer + 2),)
    two_o = ((0, outer - 4), (planes - outer + 4, planes))
    cuts = [outer - 4 + (planes - 2 * outer + 8) * i // TAILS for i in range(TAILS + 1)]

    def section(weight, ranges, maps, base_map, final=False, tips=False):
        q_map, left_map, right_map = maps
        return section_task(
            (table, 0 if weight == 1.0 else trig_values.shape[0] // 2, radius, whi, wlo), weight * courant, ranges, q_map, base_map, left_map,
            right_map, flags, planes, dims, final, tips,
        )

    edge_o, tip_one, tip_two = edges_task(span_outer, True, flags, conserved, sent_outer, dims)
    q_map = listed((conserved, sent_outer), ro)
    q_map["tips"] = near_tips + trade_tips(tip_one, tip_two)
    lefts = listed(inner_rows, ((0, planes),))
    rights = listed(lax.ppermute(edge_o, "ang", beside), ro)
    f_o, left_f, right_f, tip_one, tip_two = section(1.0, one_o, (q_map, lefts, rights), None, tips=True)
    halo_left, halo_right = trade(left_f, right_f)
    f_map = listed(f_o, one_o)
    f_map["tips"] = trade_tips(tip_one, tip_two)
    f_lefts, f_rights = listed(halo_left, one_o), listed(halo_right, one_o)

    (edge_i,) = edges_task(span_inner, False, flags, conserved, sent_inner, dims)
    q_map.update(listed((conserved, sent_inner), ri))
    rights.update(listed(lax.ppermute(edge_i, "ang", beside), ri))

    def give_back(near, far):
        return near, lax.ppermute(far, "ang", across)

    backs = []
    near, far = section(0.5, two_o, (f_map, f_lefts, f_rights), q_map, final=True)
    backs.append((two_o, give_back(near, far)))

    f_i, left_f, right_f = section(1.0, one_i, (q_map, lefts, rights), None)
    halo_left, halo_right = trade(left_f, right_f)
    f_map.update(listed(f_i, one_i))
    f_lefts.update(listed(halo_left, one_i))
    f_rights.update(listed(halo_right, one_i))
    for i in range(TAILS):
        ranges = ((cuts[i], cuts[i + 1]),)
        near, far = section(0.5, ranges, (f_map, f_lefts, f_rights), q_map, final=True)
        backs.append((ranges, give_back(near, far)))

    out = None
    for ranges, arrived in backs:
        spans = tuple((a, b - a) for a, b in ranges)
        out = place_task(spans, flags, *arrived, out, conserved.shape)
    return out


def solution(mesh):
    placed = (P(None, "ax", "ang", None), P(), P())

    return jax.shard_map(
        per_device,
        mesh=mesh,
        in_specs=placed,
        out_specs=P(None, "ax", "ang", None),
        check_vma=False,
    )
```
